256 devices in a mesh: sky: 8 (over z), tm: 32 (over x, y, core).
Axes of the slice: x: 4, y: 4, z: 8, core: 2. Of those that a mesh axis runs over, the one named last changes fastest.
Arguments:
- tiles: float32 [4096, 128, 256], P(('sky', 'tm')), may hold values from -0.375 to 0.375
- tile_seg: int32 [4096], P(('sky', 'tm')), may hold values from 0 to 511, as said below
- tile_count: int32 [4096], P(('sky', 'tm')), may hold values from 32 to 128
- src_index: int32 [4096, 128], P(('sky', 'tm')), may hold values from 0 to 131071, as said below
- src_coef: float32 [5, 4096, 128], P(None, ('sky', 'tm')), may hold values from -6 to 6
- obs_weight: float32 [4096, 128], P(('sky', 'tm')), may hold values from 0.2 to 5
- att_dir: float32 [512, 256], P('tm'), may hold values from -6 to 6
- src_dir: float32 [5, 1048576], P(None, ('sky', 'tm')), may hold values from -6 to 6
Outputs:
- projected: float32 [4096, 128], P(('sky', 'tm'))
- att_normal: float32 [512, 256], P('tm')
- src_normal: float32 [5, 1048576], P(None, ('sky', 'tm'))
- curvature: float32 [], replicated
The draws below stay inside these ranges and needn't reach their ends.
Inputs may be any that keep to these rules, and one draw needn't show every extreme that they name: `tile_seg`: within each aligned block of 16 tiles, at most 2 tiles name segments s with s // 16 equal to any one value; every block reaches 2 for some value. `src_index`: within each aligned block of 16 tiles, at most 128 observations name sources i with i // 4096 equal to any one value; every block reaches 128 for some value.
All inputs are finite; a program needn't handle non-finite values.
Results may differ from the reference program's by a relative error of at most 0.00011.
Values sent between devices are 32-bit elements; how exact they have to be, the bound alone decides.
A program may use at most 192 MiB of HBM per device.

```python
import math
import jax
import jax.numpy as jnp
from jax import lax

ROWS = 128
COLS = 256
PARAMS = 5
TILES_DEV = 16
SEG_DEV = 16
SRC_DEV = 4096
TILES = 4096
SEGMENTS = 512
SRC_G = 131072
SOURCES = 1048576
CAP_T = 2
CAP_S = 128
N_SKY = 8
N_TM = 32


def owner_block(key, full, count, n_owner, cap):
    rest = count - cap
    slots = jax.random.permutation(key, (n_owner - 1) * cap)[:rest]
    other = (slots // cap).astype(jnp.int32)
    other = other + (other >= full).astype(jnp.int32)
    owners = jnp.concatenate([jnp.full((cap,), full, dtype=jnp.int32), other])
    order = jax.random.permutation(jax.random.fold_in(key, 7), count)
    return owners[order]


def block_owners(key, salt, count, cap):
    blocks = N_SKY * N_TM
    block_ids = jnp.arange(blocks, dtype=jnp.int32)

    def one_block(block):
        sky = block // N_TM
        full = jax.random.randint(jax.random.fold_in(jax.random.fold_in(key, salt + 1), sky), (), 0, N_TM).astype(jnp.int32)
        inner = jax.random.fold_in(jax.random.fold_in(key, salt), block)
        return owner_block(inner, full, count, N_TM, cap)
    return jax.vmap(one_block)(block_ids)


def draw_tile_seg(key, part):
    owners = block_owners(key, 100, TILES_DEV, CAP_T)
    first = jax.random.randint(jax.random.fold_in(key, 200), owners.shape, 0, SEG_DEV)
    second = jax.random.randint(jax.random.fold_in(key, 201), owners.shape, 0, SEG_DEV)
    local = jnp.minimum(first, second).astype(jnp.int32)
    return (owners * SEG_DEV + local).reshape(TILES).astype(jnp.int32)


def draw_src_index(key, part):
    owners = block_owners(key, 300, TILES_DEV * ROWS, CAP_S)
    local = jax.random.randint(jax.random.fold_in(key, 400), owners.shape, 0, SRC_DEV).astype(jnp.int32)
    return (owners * SRC_DEV + local).reshape(TILES, ROWS).astype(jnp.int32)


def plant(result, stream_key, least, top_value):
    longest = result.shape.index(max(result.shape))
    spots = []
    for shift in (0, 1):
        where = [jax.random.randint(jax.random.fold_in(stream_key, axis), (), 0, length) for axis, length in enumerate(result.shape)]
        where[longest] = (where[longest] + shift) % result.shape[longest]
        spots.append(tuple(where))
    return result.at[spots[0]].set(least).at[spots[1]].set(top_value)


def steps_of(own_key, extent, pieces, low, top_value):
    gain, own = 1.0, jax.random.fold_in(own_key, 6)
    for dim, parts in pieces:
        draws = jnp.exp(jax.random.uniform(jax.random.fold_in(own, dim), (parts,), jnp.float32, low / len(pieces), top_value / len(pieces)))
        gain = gain * jnp.repeat(draws, extent[dim] // parts).reshape([-1 if axis == dim else 1 for axis in range(len(extent))])
    return gain


def gaussian(key, dims, width, bound, split=(), kind=jnp.bfloat16):
    factor_of = steps_of(key, dims, split, -0.22, 0.18) if split else 1.0
    entries = jax.random.normal(key, dims, jnp.float32) * width * factor_of
    return jnp.minimum(jnp.maximum(entries, -bound), bound).astype(kind)


def setup_inputs(seed: int = 0) -> dict:
    splits = jax.random.split(jax.random.key(seed), 9)
    tiles = gaussian(splits[0], (TILES, ROWS, COLS), COLS ** -0.5, 0.375, ((0, 256),), jnp.float32)
    tile_seg = draw_tile_seg(jax.random.fold_in(splits[8], 71), 0)
    tile_count = plant(jax.random.randint(splits[2], (TILES,), ROWS // 4, ROWS + 1), jax.random.fold_in(splits[2], 1), ROWS // 4, ROWS).astype(jnp.int32)
    src_index = draw_src_index(jax.random.fold_in(splits[8], 71), 0)
    src_coef = gaussian(splits[4], (PARAMS, TILES, ROWS), 1.0, 6.0, ((1, 256),), jnp.float32)
    obs_weight = jnp.clip(jnp.exp(math.log(5.0) - 3.218876 * jax.random.uniform(splits[5], (TILES, ROWS), jnp.float32) ** steps_of(splits[5], (TILES, ROWS), ((0, 256),), -0.2, 0.2)), 0.2, 5.0)
    att_dir = gaussian(splits[6], (SEGMENTS, COLS), 1.0, 6.0, ((0, 32),), jnp.float32)
    src_dir = gaussian(splits[7], (PARAMS, SOURCES), 1.0, 6.0, ((1, 256),), jnp.float32)
    return dict(tiles=tiles, tile_seg=tile_seg, tile_count=tile_count, src_index=src_index, src_coef=src_coef, obs_weight=obs_weight, att_dir=att_dir, src_dir=src_dir)


def reference(tiles, tile_seg, tile_count, src_index, src_coef, obs_weight, att_dir, src_dir):
    row_ids = jnp.arange(ROWS, dtype=jnp.int32)
    live_rows = row_ids[None, :] < tile_count[:, None]
    seg_rows = att_dir[tile_seg]
    att_part = jnp.einsum('tjc,tc->tj', tiles, seg_rows, precision=lax.Precision.HIGHEST)
    sky_group = (jnp.arange(TILES, dtype=jnp.int32) // (TILES_DEV * N_TM)).astype(jnp.int32)
    src_column = sky_group[:, None] * SRC_G + src_index
    picked = src_dir[:, src_column]
    projected = jnp.where(live_rows, att_part + jnp.sum(src_coef * picked, axis=0), jnp.zeros_like(att_part))
    weighted = obs_weight * projected
    curvature = jnp.sum(projected * weighted)
    tile_grad = jnp.einsum('tjc,tj->tc', tiles, weighted, precision=lax.Precision.HIGHEST)
    att_normal = jax.ops.segment_sum(tile_grad, tile_seg, num_segments=SEGMENTS)
    terms = (src_coef * weighted[None]).reshape(PARAMS, -1).T
    src_normal = jax.ops.segment_sum(terms, src_column.reshape(-1), num_segments=SOURCES).T
    return (projected, att_normal, src_normal, curvature)
```

```python
import functools

import jax
import jax.numpy as jnp
from jax import lax
from jax.experimental import pallas as pl
from jax.experimental.pallas import tpu as pltpu
from jax.sharding import PartitionSpec as P

LANES = 128
ROWS_MSG = 8
SLOT_T = 2
F32, BF16, I32 = jnp.float32, jnp.bfloat16, jnp.int32
NT = (((1,), (1,)), ((), ()))
TN = (((0,), (0,)), ((), ()))


def halves(x):
    hi = x.astype(BF16)
    return hi, (x - hi.astype(F32)).astype(BF16)


def iota(shape, dim):
    return lax.broadcasted_iota(I32, shape, dim)


def lanes_of(row, index):
    return jnp.take_along_axis(jnp.broadcast_to(row, index.shape), index, axis=1)


def kernel(
    n_sky, n_tm,
    seg_ref, cnt_ref, tiles_hbm, idx_hbm, coef_hbm, wgt_hbm, att_hbm, src_hbm,
    proj_o, att_o, src_o, curv_o,
    tiles_v, idx_v, coef_v, wgt_v, att_v, src_v, thi, tlo, low_v, dir_v, rank_v, inv_v,
    s1, r1, s2, r2, s3, r3, sz, rz,
    in_sem, send_sem, recv_sem,
):
    params, td, _ = coef_v.shape
    seg_dev, cols = att_v.shape
    src_dev = src_v.shape[1]
    nb = n_tm
    chunks = src_dev // LANES
    half = cols // LANES
    me, z = lax.axis_index("tm"), lax.axis_index("sky")

    loads = [
        pltpu.make_async_copy(a, b, in_sem.at[i])
        for i, (a, b) in enumerate(
            ((idx_hbm, idx_v), (coef_hbm, coef_v), (src_hbm, src_v), (att_hbm, att_v),
             (wgt_hbm, wgt_v), (tiles_hbm, tiles_v))
        )
    ]
    for copy in loads:
        copy.start()

    barrier = pltpu.get_barrier_semaphore()

    @pl.loop(1, n_tm)
    def _(i):
        pl.semaphore_signal(barrier, 1, device_id=(z, lax.rem(me + i, n_tm)))

    @pl.loop(1, n_sky)
    def _(i):
        pl.semaphore_signal(barrier, 1, device_id=(lax.rem(z + i, n_sky), me))

    def strided(ref, row):
        return ref[pl.ds(row, nb, stride=ROWS_MSG), :]

    def put(ref, row, value):
        ref[pl.ds(row, nb, stride=ROWS_MSG), :] = value

    def block(q):
        return pl.ds(pl.multiple_of(q * ROWS_MSG, ROWS_MSG), ROWS_MSG)

    def exchange(src, dst, k):
        @pl.loop(1, n_tm)
        def _(i):
            q = lax.rem(me + i, n_tm)
            pltpu.make_async_remote_copy(
                src_ref=src.at[block(q)], dst_ref=dst.at[block(me)],
                send_sem=send_sem.at[k], recv_sem=recv_sem.at[k],
                device_id=(z, q), device_id_type=pl.DeviceIdType.MESH,
            ).start()

        dst[block(me), :] = src[block(me), :]

    def await_bytes(ref, rows, sem):
        view = ref.at[pl.ds(0, rows)]
        pltpu.make_async_copy(view, view, sem).wait()

    seg_shift = seg_dev.bit_length() - 1
    owner_t = [seg_ref[t] >> seg_shift for t in range(td)]
    local_t = [seg_ref[t] & (seg_dev - 1) for t in range(td)]
    rank_t = []
    for t in range(td):
        r = jnp.int32(0)
        for before in range(t):
            r = r + (owner_t[before] == owner_t[t]).astype(I32)
        rank_t.append(r)
    bins, lane = iota((nb, LANES), 0), iota((nb, LANES), 1)
    wanted = jnp.zeros((nb, LANES), I32)
    for t in range(td):
        hit = (bins == owner_t[t]) & (lane == rank_t[t])
        wanted = jnp.where(hit, local_t[t] + 1, wanted)

    loads[0].wait()
    src_shift = src_dev.bit_length() - 1
    idx = idx_v[...]
    owner = idx >> src_shift
    mine = [jnp.broadcast_to(owner[t : t + 1], (nb, LANES)) == bins for t in range(td)]
    ones = [m.astype(F32) for m in mine]
    i0, i1 = iota((LANES, 2 * LANES), 0), iota((LANES, 2 * LANES), 1)
    tri = ((i0 < i1) | (i1 >= LANES)).astype(F32).astype(BF16)
    counts = jnp.dot(
        jnp.concatenate(ones, axis=0).astype(BF16), tri, preferred_element_type=F32
    )
    offset = jnp.zeros((nb, LANES), F32)
    slot_id = iota((LANES, LANES), 0)
    spots, origin = [], []
    lane_f = lane.astype(F32)
    for t in range(td):
        here = counts[t * nb : (t + 1) * nb]
        rank = jnp.sum(jnp.where(mine[t], here[:, :LANES] + offset, 0.0), axis=0, keepdims=True)
        rank = rank.astype(I32)
        offset = offset + here[:, LANES:]
        rank_v[t : t + 1, :] = rank
        spots.append((jnp.broadcast_to(rank, (LANES, LANES)) == slot_id).astype(F32).astype(BF16))
        origin.append(jnp.concatenate([ones[t] * (t + 1.0), ones[t] * lane_f], axis=0).astype(BF16))
    found = lax.dot_general(
        jnp.concatenate(origin, axis=1), jnp.concatenate(spots, axis=1), NT,
        preferred_element_type=F32,
    ).astype(I32)
    inv_v[...] = found

    def to_slots(rows):
        tile, col = inv_v[:nb, :], inv_v[nb:, :]
        out = jnp.zeros((nb, LANES), F32)
        for t in range(td):
            out = jnp.where(tile == t + 1, lanes_of(rows[t : t + 1], col), out)
        return out

    loads[1].wait()
    for k in range(params):
        put(s1, k, to_slots(coef_v[k]))
    put(s1, params, to_slots((idx & (src_dev - 1)).astype(F32)))
    put(s1, params + 1, wanted.astype(F32))
    put(s1, params + 2, jnp.zeros((nb, LANES), F32))

    pl.semaphore_wait(barrier, n_tm + n_sky - 2)
    exchange(s1, r1, 0)

    loads[5].wait()

    @pl.loop(0, td)
    def _(t):
        rows = pl.ds(pl.multiple_of(t * LANES, LANES), LANES)
        hi, lo = halves(tiles_v[t])
        thi[rows, :] = hi
        tlo[rows, :] = lo

    for copy in (loads[2], loads[3], loads[4]):
        copy.wait()

    await_bytes(r1, (n_tm - 1) * ROWS_MSG, recv_sem.at[0])

    asked = strided(r1, params).astype(I32)
    chunk, col = asked >> 7, asked & (LANES - 1)
    picked = [jnp.zeros((nb, LANES), F32) for _ in range(params)]
    for h in range(chunks):
        here = chunk == h
        for k in range(params):
            row = src_v[k : k + 1, h * LANES : (h + 1) * LANES]
            picked[k] = jnp.where(here, lanes_of(row, col), picked[k])
    total = jnp.zeros((nb, LANES), F32)
    for k in range(params):
        total = total + strided(r1, k) * picked[k]
    put(s2, 0, total)
    segs = strided(r1, params + 1).astype(I32)
    seg_id = iota((nb, seg_dev), 1) + 1
    att_pair = jnp.concatenate(halves(att_v[...]), axis=1)
    choice = []
    for r in range(SLOT_T):
        pick = jnp.broadcast_to(segs[:, r : r + 1], (nb, seg_dev)) == seg_id
        choice.append(pick.astype(F32).astype(BF16))
        both = jnp.dot(choice[r], att_pair, preferred_element_type=F32)
        rows = both[:, :cols] + both[:, cols:]
        for c in range(half):
            put(s2, 1 + r * half + c, rows[:, c * LANES : (c + 1) * LANES])
    for k in range(1 + SLOT_T * half, ROWS_MSG):
        put(s2, k, jnp.zeros((nb, LANES), F32))
    exchange(s2, r2, 1)

    for p in range(nb):
        low_v[:, p * LANES : (p + 1) * LANES] = (
            jnp.broadcast_to(col[p : p + 1], (LANES, LANES)) == slot_id
        ).astype(F32).astype(BF16)
    obs_t, obs_row = iota((td, LANES), 0), iota((td, LANES), 1)
    count = jnp.zeros((td, LANES), I32)
    for t in range(td):
        count = jnp.where(obs_t == t, cnt_ref[t], count)
    live = obs_row < count

    await_bytes(r2, (n_tm - 1) * ROWS_MSG, recv_sem.at[1])

    for t in range(td):
        for c in range(half):
            dir_v[t : t + 1, c * LANES : (c + 1) * LANES] = r2[
                pl.ds(owner_t[t] * ROWS_MSG + 1 + rank_t[t] * half + c, 1), :
            ]
    dir_hi, dir_lo = halves(dir_v[...])
    first = lax.dot_general(
        jnp.concatenate([dir_hi, dir_lo], axis=0), thi[...], NT, preferred_element_type=F32
    )
    second = lax.dot_general(dir_hi, tlo[...], NT, preferred_element_type=F32)
    sums = first[:td] + first[td:] + second
    part = jnp.zeros((td, LANES), F32)
    for t in range(td):
        part = jnp.where(obs_t == t, sums[:, t * LANES : (t + 1) * LANES], part)
    answers = strided(r2, 0)
    rank = rank_v[...]
    source = jnp.zeros((td, LANES), F32)
    for b in range(nb):
        source = jnp.where(owner == b, lanes_of(answers[b : b + 1], rank), source)
    projected = jnp.where(live, part + source, 0.0)
    proj_o[...] = projected
    weighted = wgt_v[...] * projected
    curvature = jnp.sum(projected * weighted)

    put(s3, 0, to_slots(weighted))
    w_hi, w_lo = halves(weighted)
    w_hi, w_lo = w_hi.astype(F32), w_lo.astype(F32)
    slots = iota((SLOT_T * nb, LANES), 0)
    left = []
    for t in range(td):
        here = slots == rank_t[t] * nb + owner_t[t]
        left.append(
            jnp.concatenate(
                [
                    jnp.where(here, jnp.broadcast_to(w[t : t + 1], slots.shape), 0.0)
                    for w in (w_hi, w_lo)
                ],
                axis=0,
            ).astype(BF16)
        )
    left = jnp.concatenate(left, axis=1)
    n_slots = SLOT_T * nb
    grad = jnp.dot(left, thi[...], preferred_element_type=F32)
    grad = (
        grad[:n_slots]
        + grad[n_slots:]
        + jnp.dot(left[:n_slots], tlo[...], preferred_element_type=F32)
    )
    for r in range(SLOT_T):
        for c in range(half):
            put(
                s3, 1 + r * half + c,
                grad[r * nb : (r + 1) * nb, c * LANES : (c + 1) * LANES],
            )
    put(s3, 1 + SLOT_T * half, jnp.full((nb, LANES), curvature, F32))
    for k in range(2 + SLOT_T * half, ROWS_MSG):
        put(s3, k, jnp.zeros((nb, LANES), F32))
    exchange(s3, r3, 2)
    await_bytes(r3, (n_tm - 1) * ROWS_MSG, recv_sem.at[2])

    zrows = seg_dev * half + 8

    def zblock(q):
        return pl.ds(pl.multiple_of(q * zrows, 8), zrows)

    owned = jnp.zeros((seg_dev, cols), F32)
    for r in range(SLOT_T):
        rows = jnp.concatenate([strided(r3, 1 + r * half + c) for c in range(half)], axis=1)
        both = lax.dot_general(
            choice[r], jnp.concatenate(halves(rows), axis=1), TN, preferred_element_type=F32
        )
        owned = owned + both[:, :cols] + both[:, cols:]
    for c in range(half):
        sz[c * seg_dev : (c + 1) * seg_dev, :] = owned[:, c * LANES : (c + 1) * LANES]
    curv_rows = jnp.sum(strided(r3, 1 + SLOT_T * half), axis=0, keepdims=True)
    sz[seg_dev * half : zrows, :] = jnp.broadcast_to(curv_rows, (8, LANES))

    @pl.loop(1, n_sky)
    def _(i):
        q = lax.rem(z + i, n_sky)
        pltpu.make_async_remote_copy(
            src_ref=sz, dst_ref=rz.at[zblock(z)],
            send_sem=send_sem.at[3], recv_sem=recv_sem.at[3],
            device_id=(q, me), device_id_type=pl.DeviceIdType.MESH,
        ).start()

    rz[zblock(z), :] = sz[...]

    back = strided(r3, 0)
    chunk_id = iota((chunks, LANES), 0)
    terms = []
    for k in range(params):
        hi, lo = halves(strided(r1, k) * back)
        terms.append((hi.astype(F32), lo.astype(F32)))
    grid = []
    for p in range(nb):
        here = jnp.broadcast_to(chunk[p : p + 1], chunk_id.shape) == chunk_id
        grid.append(
            jnp.concatenate(
                [
                    jnp.where(here, jnp.broadcast_to(terms[k][i][p : p + 1], here.shape), 0.0)
                    for i in range(2)
                    for k in range(params)
                ],
                axis=0,
            ).astype(BF16)
        )
    both = lax.dot_general(
        jnp.concatenate(grid, axis=1), low_v[...], NT, preferred_element_type=F32
    )
    rows = params * chunks
    spread = both[:rows] + both[rows:]
    for k in range(params):
        for h in range(chunks):
            src_o[k : k + 1, h * LANES : (h + 1) * LANES] = spread[
                k * chunks + h : k * chunks + h + 1
            ]

    await_bytes(rz, (n_sky - 1) * zrows, recv_sem.at[3])
    summed = rz[0:zrows, :]
    for q in range(1, n_sky):
        summed = summed + rz[q * zrows : (q + 1) * zrows, :]
    for c in range(half):
        att_o[:, c * LANES : (c + 1) * LANES] = summed[c * seg_dev : (c + 1) * seg_dev]
    curv_o[0] = summed[seg_dev * half, 0]

    for k, ref in enumerate((s1, s2, s3)):
        await_bytes(ref, (n_tm - 1) * ROWS_MSG, send_sem.at[k])
    await_bytes(rz, (n_sky - 1) * zrows, send_sem.at[3])


def per_device(n_sky, n_tm, tiles, tile_seg, tile_count, src_index, src_coef, obs_weight, att_dir, src_dir):
    td, rows, cols = tiles.shape
    params, src_dev = src_dir.shape
    seg_dev = att_dir.shape[0]
    msg = pltpu.VMEM((n_tm * ROWS_MSG, LANES), F32)
    zrows = seg_dev * (cols // LANES) + 8
    vmem, smem, hbm = (
        pl.BlockSpec(memory_space=s) for s in (pltpu.VMEM, pltpu.SMEM, pl.ANY)
    )
    projected, att_normal, src_normal, curvature = pl.pallas_call(
        functools.partial(kernel, n_sky, n_tm),
        out_shape=(
            jax.ShapeDtypeStruct((td, rows), F32),
            jax.ShapeDtypeStruct((seg_dev, cols), F32),
            jax.ShapeDtypeStruct((params, src_dev), F32),
            jax.ShapeDtypeStruct((1,), F32),
        ),
        in_specs=[smem, smem, hbm, hbm, hbm, hbm, hbm, hbm],
        out_specs=(vmem, vmem, vmem, smem),
        scratch_shapes=[
            pltpu.VMEM((td, rows, cols), F32),
            pltpu.VMEM((td, rows), I32),
            pltpu.VMEM((params, td, rows), F32),
            pltpu.VMEM((td, rows), F32),
            pltpu.VMEM((seg_dev, cols), F32),
            pltpu.VMEM((params, src_dev), F32),
            pltpu.VMEM((td * rows, cols), BF16),
            pltpu.VMEM((td * rows, cols), BF16),
            pltpu.VMEM((LANES, n_tm * LANES), BF16),
            pltpu.VMEM((td, cols), F32),
            pltpu.VMEM((td, rows), I32),
            pltpu.VMEM((2 * n_tm, LANES), I32),
            msg, msg, msg, msg, msg, msg,
            pltpu.VMEM((zrows, LANES), F32),
            pltpu.VMEM((n_sky * zrows, LANES), F32),
            pltpu.SemaphoreType.DMA((6,)),
            pltpu.SemaphoreType.DMA((4,)),
            pltpu.SemaphoreType.DMA((4,)),
        ],
        compiler_params=pltpu.CompilerParams(
            collective_id=0, has_side_effects=True, vmem_limit_bytes=48 << 20
        ),
    )(tile_seg, tile_count, tiles, src_index, src_coef, obs_weight, att_dir, src_dir)
    return projected, att_normal, src_normal, curvature.reshape(())


def solution(mesh):
    placed = (
        P(("sky", "tm"), None, None),
        P(("sky", "tm")),
        P(("sky", "tm")),
        P(("sky", "tm"), None),
        P(None, ("sky", "tm"), None),
        P(("sky", "tm"), None),
        P("tm", None),
        P(None, ("sky", "tm")),
    )
    return jax.shard_map(
        functools.partial(per_device, mesh.shape["sky"], mesh.shape["tm"]),
        mesh=mesh,
        in_specs=placed,
        out_specs=(P(("sky", "tm"), None), P("tm", None), P(None, ("sky", "tm")), P()),
        check_vma=False,
    )
```

```python
import functools

import jax
import jax.numpy as jnp
from jax import lax
from jax.experimental import pallas as pl
from jax.experimental.pallas import tpu as pltpu
from jax.sharding import PartitionSpec as P

LANES = 128
ROWS_MSG = 8
GROUP = 8
SCOPED = 58 << 20
SLOT_T = 2
F32, BF16, I32 = jnp.float32, jnp.bfloat16, jnp.int32
NT = (((1,), (1,)), ((), ()))
TN = (((0,), (0,)), ((), ()))


def halves(x):
    hi = x.astype(BF16)
    return hi, (x - hi.astype(F32)).astype(BF16)


def iota(shape, dim):
    return lax.broadcasted_iota(I32, shape, dim)


def lanes_of(row, index):
    return jnp.take_along_axis(jnp.broadcast_to(row, index.shape), index, axis=1)


def hops(step, extents):
    total = 0
    for n in reversed(extents):
        part = step % n
        step //= n
        total += min(part, n - part)
    return total


def kernel(
    n_sky, n_tm,
    seg_ref, cnt_ref, tiles_hbm, idx_hbm, coef_hbm, wgt_hbm, att_hbm, src_hbm,
    proj_o, sums_o, src_o,
    tiles_v, idx_v, coef_v, wgt_v, att_v, src_v, thi, tlo, low_v, dir_v, rank_v, inv_v,
    s1, r1, s2, r2, s3, r3, sz, rz,
    in_sem, send_sem, recv_sem, zsend_sem, zrecv_sem,
):
    params, td, _ = coef_v.shape
    seg_dev, cols = att_v.shape
    src_dev = src_v.shape[1]
    nb = n_tm
    groups = n_tm // GROUP
    chunks = src_dev // LANES
    half = cols // LANES
    me, z = lax.axis_index("tm"), lax.axis_index("sky")
    my_group = me // GROUP
    across = sorted(range(groups), key=lambda k: -min(k, groups - k))
    within = sorted(range(GROUP), key=lambda k: -hops(k, (4, 2)))

    loads = [
        pltpu.make_async_copy(a, b, in_sem.at[i])
        for i, (a, b) in enumerate(
            ((idx_hbm, idx_v), (coef_hbm, coef_v), (src_hbm, src_v), (att_hbm, att_v),
             (wgt_hbm, wgt_v), (tiles_hbm, tiles_v))
        )
    ]
    for copy in loads:
        copy.start()

    barrier = pltpu.get_barrier_semaphore()

    @pl.loop(1, n_tm)
    def _(i):
        pl.semaphore_signal(barrier, 1, device_id=(z, jnp.bitwise_xor(me, i)))

    @pl.loop(1, n_sky)
    def _(i):
        pl.semaphore_signal(barrier, 1, device_id=(lax.rem(z + i, n_sky), me))

    def strided(ref, row):
        return ref[pl.ds(row, nb, stride=ROWS_MSG), :]

    def put(ref, row, value):
        ref[pl.ds(row, nb, stride=ROWS_MSG), :] = value

    def group_start(k):
        return pl.multiple_of(jnp.bitwise_xor(my_group, k) * (GROUP * ROWS_MSG), GROUP * ROWS_MSG)

    def strided_group(ref, row, k):
        return ref[pl.ds(group_start(k) + row, GROUP, stride=ROWS_MSG), :]

    def put_group(ref, row, k, value):
        ref[pl.ds(group_start(k) + row, GROUP, stride=ROWS_MSG), :] = value

    def block(q, first, rows):
        return pl.ds(pl.multiple_of(q * ROWS_MSG, ROWS_MSG) + first, rows)

    def send_group(src, dst, phase, k, first, rows):
        for j in within:
            step = k * GROUP + j
            if step == 0:
                continue
            q = jnp.bitwise_xor(me, step)
            pltpu.make_async_remote_copy(
                src_ref=src.at[block(q, first, rows)], dst_ref=dst.at[block(me, first, rows)],
                send_sem=send_sem.at[phase], recv_sem=recv_sem.at[phase, k],
                device_id=(z, q), device_id_type=pl.DeviceIdType.MESH,
            ).start()

    def keep(src, dst):
        dst[block(me, 0, ROWS_MSG), :] = src[block(me, 0, ROWS_MSG), :]

    def await_bytes(ref, rows, sem):
        view = ref.at[pl.ds(0, rows)]
        pltpu.make_async_copy(view, view, sem).wait()

    def await_group(ref, phase, k, rows):
        await_bytes(ref, (GROUP - (k == 0)) * rows, recv_sem.at[phase, k])

    seg_shift = seg_dev.bit_length() - 1
    owner_t = [seg_ref[t] >> seg_shift for t in range(td)]
    local_t = [seg_ref[t] & (seg_dev - 1) for t in range(td)]
    rank_t = []
    for t in range(td):
        r = jnp.int32(0)
        for before in range(t):
            r = r + (owner_t[before] == owner_t[t]).astype(I32)
        rank_t.append(r)
    bins, lane = iota((nb, LANES), 0), iota((nb, LANES), 1)
    wanted = jnp.zeros((nb, LANES), I32)
    for t in range(td):
        hit = (bins == owner_t[t]) & (lane == rank_t[t])
        wanted = jnp.where(hit, local_t[t] + 1, wanted)
    put(s1, params + 1, wanted.astype(F32))

    loads[0].wait()
    src_shift = src_dev.bit_length() - 1
    idx = idx_v[...]
    owner = idx >> src_shift
    mine = [jnp.broadcast_to(owner[t : t + 1], (nb, LANES)) == bins for t in range(td)]
    ones = [m.astype(F32) for m in mine]
    i0, i1 = iota((LANES, 2 * LANES), 0), iota((LANES, 2 * LANES), 1)
    tri = ((i0 < i1) | (i1 >= LANES)).astype(F32).astype(BF16)
    counts = jnp.dot(
        jnp.concatenate(ones, axis=0).astype(BF16), tri, preferred_element_type=F32
    )
    offset = jnp.zeros((nb, LANES), F32)
    slot_id = iota((LANES, LANES), 0)
    spots, origin = [], []
    lane_f = lane.astype(F32)
    for t in range(td):
        here = counts[t * nb : (t + 1) * nb]
        rank = jnp.sum(jnp.where(mine[t], here[:, :LANES] + offset, 0.0), axis=0, keepdims=True)
        rank = rank.astype(I32)
        offset = offset + here[:, LANES:]
        rank_v[t : t + 1, :] = rank
        spots.append((jnp.broadcast_to(rank, (LANES, LANES)) == slot_id).astype(F32).astype(BF16))
        origin.append(jnp.concatenate([ones[t] * (t + 1.0), ones[t] * lane_f], axis=0).astype(BF16))
    found = lax.dot_general(
        jnp.concatenate(origin, axis=1), jnp.concatenate(spots, axis=1), NT,
        preferred_element_type=F32,
    ).astype(I32)
    inv_v[...] = found

    def to_slots(rows):
        tile, col = inv_v[:nb, :], inv_v[nb:, :]
        out = jnp.zeros((nb, LANES), F32)
        for t in range(td):
            out = jnp.where(tile == t + 1, lanes_of(rows[t : t + 1], col), out)
        return out

    loads[1].wait()
    for k in range(params):
        put(s1, k, to_slots(coef_v[k]))
    put(s1, params, to_slots((idx & (src_dev - 1)).astype(F32)))

    asked_rows = params + 2
    pl.semaphore_wait(barrier, n_tm + n_sky - 2)
    for k in across:
        send_group(s1, r1, 0, k, 0, asked_rows)
    keep(s1, r1)

    loads[5].wait()

    @pl.loop(0, td)
    def _(t):
        rows = pl.ds(pl.multiple_of(t * LANES, LANES), LANES)
        hi, lo = halves(tiles_v[t])
        thi[rows, :] = hi
        tlo[rows, :] = lo

    for copy in (loads[2], loads[3], loads[4]):
        copy.wait()
    att_pair = jnp.concatenate(halves(att_v[...]), axis=1)
    obs_t, obs_row = iota((td, LANES), 0), iota((td, LANES), 1)
    count = jnp.zeros((td, LANES), I32)
    for t in range(td):
        count = jnp.where(obs_t == t, cnt_ref[t], count)
    live = obs_row < count

    answer_rows = 1 + SLOT_T * half
    seg_id = iota((GROUP, seg_dev), 1) + 1
    for k in reversed(across):
        await_group(r1, 0, k, asked_rows)
        asked = strided_group(r1, params, k).astype(I32)
        chunk, col = asked >> 7, asked & (LANES - 1)
        picked = [jnp.zeros((GROUP, LANES), F32) for _ in range(params)]
        for h in range(chunks):
            here = chunk == h
            for p in range(params):
                row = src_v[p : p + 1, h * LANES : (h + 1) * LANES]
                picked[p] = jnp.where(here, lanes_of(row, col), picked[p])
        total = jnp.zeros((GROUP, LANES), F32)
        for p in range(params):
            total = total + strided_group(r1, p, k) * picked[p]
        put_group(s2, 0, k, total)
        segs = strided_group(r1, params + 1, k).astype(I32)
        pick = jnp.concatenate(
            [
                jnp.broadcast_to(segs[:, r : r + 1], (GROUP, seg_dev)) == seg_id
                for r in range(SLOT_T)
            ],
            axis=0,
        ).astype(F32).astype(BF16)
        both = jnp.dot(pick, att_pair, preferred_element_type=F32)
        rows = both[:, :cols] + both[:, cols:]
        for r in range(SLOT_T):
            for c in range(half):
                put_group(
                    s2, 1 + r * half + c, k,
                    rows[r * GROUP : (r + 1) * GROUP, c * LANES : (c + 1) * LANES],
                )
        send_group(s2, r2, 1, k, 0, answer_rows)
    keep(s2, r2)

    asked = strided(r1, params).astype(I32)
    chunk, col = asked >> 7, asked & (LANES - 1)
    for p in range(nb):
        low_v[:, p * LANES : (p + 1) * LANES] = (
            jnp.broadcast_to(col[p : p + 1], (LANES, LANES)) == slot_id
        ).astype(F32).astype(BF16)
    segs = strided(r1, params + 1).astype(I32)
    choice = jnp.concatenate(
        [
            jnp.broadcast_to(segs[:, r : r + 1], (nb, seg_dev)) == iota((nb, seg_dev), 1) + 1
            for r in range(SLOT_T)
        ],
        axis=0,
    ).astype(F32).astype(BF16)

    rank = rank_v[...]
    source = jnp.zeros((td, LANES), F32)
    for k in reversed(across):
        await_group(r2, 1, k, answer_rows)
        answers = strided_group(r2, 0, k)
        first = jnp.bitwise_xor(my_group, k) * GROUP
        for w in range(GROUP):
            source = jnp.where(owner == first + w, lanes_of(answers[w : w + 1], rank), source)
    for t in range(td):
        for c in range(half):
            dir_v[t : t + 1, c * LANES : (c + 1) * LANES] = r2[
                pl.ds(owner_t[t] * ROWS_MSG + 1 + rank_t[t] * half + c, 1), :
            ]
    dir_hi, dir_lo = halves(dir_v[...])
    first = lax.dot_general(
        jnp.concatenate([dir_hi, dir_lo], axis=0), thi[...], NT, preferred_element_type=F32
    )
    second = lax.dot_general(dir_hi, tlo[...], NT, preferred_element_type=F32)
    sums = first[:td] + first[td:] + second
    part = jnp.zeros((td, LANES), F32)
    for t in range(td):
        part = jnp.where(obs_t == t, sums[:, t * LANES : (t + 1) * LANES], part)
    projected = jnp.where(live, part + source, 0.0)
    proj_o[...] = projected
    weighted = wgt_v[...] * projected
    curvature = jnp.sum(projected * weighted)

    w_hi, w_lo = halves(weighted)
    w_hi, w_lo = w_hi.astype(F32), w_lo.astype(F32)
    slots = iota((SLOT_T * nb, LANES), 0)
    left = []
    for t in range(td):
        here = slots == rank_t[t] * nb + owner_t[t]
        left.append(
            jnp.concatenate(
                [
                    jnp.where(here, jnp.broadcast_to(w[t : t + 1], slots.shape), 0.0)
                    for w in (w_hi, w_lo)
                ],
                axis=0,
            ).astype(BF16)
        )
    left = jnp.concatenate(left, axis=1)
    n_slots = SLOT_T * nb
    grad = jnp.dot(left, thi[...], preferred_element_type=F32)
    grad = (
        grad[:n_slots]
        + grad[n_slots:]
        + jnp.dot(left[:n_slots], tlo[...], preferred_element_type=F32)
    )
    for r in range(SLOT_T):
        for c in range(half):
            put(
                s3, r * half + c,
                grad[r * nb : (r + 1) * nb, c * LANES : (c + 1) * LANES],
            )
    curv_row = SLOT_T * half
    put(s3, curv_row, jnp.full((nb, LANES), curvature, F32))
    for k in across:
        send_group(s3, r3, 2, k, 0, curv_row + 1)
    weight_row = curv_row + 1
    put(s3, weight_row, to_slots(weighted))
    for k in across:
        send_group(s3, r3, 3, k, weight_row, 1)
    keep(s3, r3)
    for k in across:
        await_group(r3, 2, k, curv_row + 1)

    zrows = seg_dev * half + 1
    pitch = rz.shape[0] // n_sky

    def zblock(q):
        return pl.ds(pl.multiple_of(q * pitch, 8), zrows)

    rows = jnp.concatenate(
        [
            jnp.concatenate([strided(r3, r * half + c) for c in range(half)], axis=1)
            for r in range(SLOT_T)
        ],
        axis=0,
    )
    both = lax.dot_general(
        choice, jnp.concatenate(halves(rows), axis=1), TN, preferred_element_type=F32
    )
    owned = both[:, :cols] + both[:, cols:]
    for c in range(half):
        sz[c * seg_dev : (c + 1) * seg_dev, :] = owned[:, c * LANES : (c + 1) * LANES]
    sz[zrows - 1 : zrows, :] = jnp.sum(strided(r3, curv_row), axis=0, keepdims=True)

    for i in sorted(range(1, n_sky), key=lambda i: -min(i, n_sky - i)):
        q = lax.rem(z + i, n_sky)
        pltpu.make_async_remote_copy(
            src_ref=sz.at[pl.ds(0, zrows)], dst_ref=rz.at[zblock(z)],
            send_sem=zsend_sem.at[0], recv_sem=zrecv_sem.at[0],
            device_id=(q, me), device_id_type=pl.DeviceIdType.MESH,
        ).start()

    rz[zblock(z), :] = sz[0:zrows, :]

    for k in across:
        await_group(r3, 3, k, 1)
    back = strided(r3, weight_row)
    chunk_id = iota((chunks, LANES), 0)
    terms = []
    for k in range(params):
        hi, lo = halves(strided(r1, k) * back)
        terms.append((hi.astype(F32), lo.astype(F32)))
    grid = []
    for p in range(nb):
        here = jnp.broadcast_to(chunk[p : p + 1], chunk_id.shape) == chunk_id
        grid.append(
            jnp.concatenate(
                [
                    jnp.where(here, jnp.broadcast_to(terms[k][i][p : p + 1], here.shape), 0.0)
                    for i in range(2)
                    for k in range(params)
                ],
                axis=0,
            ).astype(BF16)
        )
    both = lax.dot_general(
        jnp.concatenate(grid, axis=1), low_v[...], NT, preferred_element_type=F32
    )
    rows = params * chunks
    spread = both[:rows] + both[rows:]
    for k in range(params):
        for h in range(chunks):
            src_o[k : k + 1, h * LANES : (h + 1) * LANES] = spread[
                k * chunks + h : k * chunks + h + 1
            ]

    for k, (ref, rows) in enumerate(
        ((s1, asked_rows), (s2, answer_rows), (s3, curv_row + 1), (s3, 1))
    ):
        await_bytes(ref, (n_tm - 1) * rows, send_sem.at[k])
    await_bytes(rz, (n_sky - 1) * zrows, zrecv_sem.at[0])
    summed = rz[0:zrows, :]
    for q in range(1, n_sky):
        summed = summed + rz[q * pitch : q * pitch + zrows, :]
    sums_o[0:zrows, :] = summed
    await_bytes(rz, (n_sky - 1) * zrows, zsend_sem.at[0])


def hand_over(proj, sums, src, proj_o, att_o, src_o, curv_o):
    seg_dev, cols = att_o.shape
    half = cols // LANES
    proj_o[...] = proj[...]
    src_o[...] = src[...]
    for c in range(half):
        att_o[:, c * LANES : (c + 1) * LANES] = sums[c * seg_dev : (c + 1) * seg_dev, :]
    curv_o[0] = sums[seg_dev * half, 0]


def per_device(n_sky, n_tm, tiles, tile_seg, tile_count, src_index, src_coef, obs_weight, att_dir, src_dir):
    td, rows, cols = tiles.shape
    params, src_dev = src_dir.shape
    seg_dev = att_dir.shape[0]
    groups = n_tm // GROUP
    msg = pltpu.VMEM((n_tm * ROWS_MSG, LANES), F32)
    pitch = seg_dev * (cols // LANES) + 8
    vmem, smem, hbm = (
        pl.BlockSpec(memory_space=s) for s in (pltpu.VMEM, pltpu.SMEM, pl.ANY)
    )
    projected, sums, src_normal = pl.pallas_call(
        functools.partial(kernel, n_sky, n_tm),
        out_shape=(
            jax.ShapeDtypeStruct((td, rows), F32),
            jax.ShapeDtypeStruct((pitch, LANES), F32),
            jax.ShapeDtypeStruct((params, src_dev), F32),
        ),
        in_specs=[smem, smem, hbm, hbm, hbm, hbm, hbm, hbm],
        out_specs=(vmem, vmem, vmem),
        scratch_shapes=[
            pltpu.VMEM((td, rows, cols), F32),
            pltpu.VMEM((td, rows), I32),
            pltpu.VMEM((params, td, rows), F32),
            pltpu.VMEM((td, rows), F32),
            pltpu.VMEM((seg_dev, cols), F32),
            pltpu.VMEM((params, src_dev), F32),
            pltpu.VMEM((td * rows, cols), BF16),
            pltpu.VMEM((td * rows, cols), BF16),
            pltpu.VMEM((LANES, n_tm * LANES), BF16),
            pltpu.VMEM((td, cols), F32),
            pltpu.VMEM((td, rows), I32),
            pltpu.VMEM((2 * n_tm, LANES), I32),
            msg, msg, msg, msg, msg, msg,
            pltpu.VMEM((pitch, LANES), F32),
            pltpu.VMEM((n_sky * pitch, LANES), F32),
            pltpu.SemaphoreType.DMA((6,)),
            pltpu.SemaphoreType.DMA((4,)),
            pltpu.SemaphoreType.DMA((4, groups)),
            pltpu.SemaphoreType.DMA((1,)),
            pltpu.SemaphoreType.DMA((1,)),
        ],
        compiler_params=pltpu.CompilerParams(
            collective_id=0, has_side_effects=True, vmem_limit_bytes=SCOPED
        ),
    )(tile_seg, tile_count, tiles, src_index, src_coef, obs_weight, att_dir, src_dir)
    projected, att_normal, src_normal, curvature = pl.pallas_call(
        hand_over,
        out_shape=(
            jax.ShapeDtypeStruct((td, rows), F32),
            jax.ShapeDtypeStruct((seg_dev, cols), F32),
            jax.ShapeDtypeStruct((params, src_dev), F32),
            jax.ShapeDtypeStruct((1,), F32),
        ),
        in_specs=[vmem, vmem, vmem],
        out_specs=(vmem, vmem, vmem, smem),
        compiler_params=pltpu.CompilerParams(vmem_limit_bytes=SCOPED),
    )(projected, sums, src_normal)
    return projected, att_normal, src_normal, curvature.reshape(())


def solution(mesh):
    placed = (
        P(("sky", "tm"), None, None),
        P(("sky", "tm")),
        P(("sky", "tm")),
        P(("sky", "tm"), None),
        P(None, ("sky", "tm"), None),
        P(("sky", "tm"), None),
        P("tm", None),
        P(None, ("sky", "tm")),
    )
    return jax.shard_map(
        functools.partial(per_device, mesh.shape["sky"], mesh.shape["tm"]),
        mesh=mesh,
        in_specs=placed,
        out_specs=(P(("sky", "tm"), None), P("tm", None), P(None, ("sky", "tm")), P()),
        check_vma=False,
    )
```

```python
import functools

import jax
import jax.numpy as jnp
from jax import lax
from jax.experimental import pallas as pl
from jax.experimental.pallas import tpu as pltpu
from jax.sharding import PartitionSpec as P

LANES = 128
ROWS_MSG = 8
GROUP = 8
SCOPED = 44 << 20
SLOT_T = 2
F32, BF16, I32 = jnp.float32, jnp.bfloat16, jnp.int32
NT = (((1,), (1,)), ((), ()))


def halves(x):
    hi = x.astype(BF16)
    return hi, (x - hi.astype(F32)).astype(BF16)


def iota(shape, dim):
    return lax.broadcasted_iota(I32, shape, dim)


def lanes_of(row, index):
    return jnp.take_along_axis(jnp.broadcast_to(row, index.shape), index, axis=1)


def hops(step, extents):
    total = 0
    for n in reversed(extents):
        part = step % n
        step //= n
        total += min(part, n - part)
    return total


def kernel(
    n_sky, n_tm,
    seg_hbm, cnt_hbm, tiles_hbm, idx_hbm, coef_hbm, wgt_hbm, att_hbm, src_hbm,
    proj_o, sums_o, src_o,
    seg_ref, cnt_ref, tiles_v, idx_v, coef_v, wgt_v, att_v, src_v, thi, tlo, thi_t, tlo_t, low_v, dir_v, rank_v, inv_v,
    s1, r1, s2, r2, s3, r3, sz, rz,
    in_sem, send_sem, recv_sem, zsend_sem, zrecv_sem,
):
    params, td, _ = coef_v.shape
    seg_dev, cols = att_v.shape
    src_dev = src_v.shape[1]
    nb = n_tm
    groups = n_tm // GROUP
    chunks = src_dev // LANES
    half = cols // LANES
    me, z = lax.axis_index("tm"), lax.axis_index("sky")
    my_group = me // GROUP
    across = sorted(range(groups), key=lambda k: -min(k, groups - k))
    within = sorted(range(GROUP), key=lambda k: -hops(k, (4, 2)))

    barrier = pltpu.get_barrier_semaphore()

    for k in across:
        for j in within:
            if k or j:
                q = jnp.bitwise_xor(me, k * GROUP + j)
                pl.semaphore_signal(barrier, 1, device_id=(z, q))

    @pl.loop(1, n_sky)
    def _(i):
        pl.semaphore_signal(barrier, 1, device_id=(lax.rem(z + i, n_sky), me))

    loads = [
        pltpu.make_async_copy(a, b, in_sem.at[i])
        for i, (a, b) in enumerate(
            ((idx_hbm, idx_v), (coef_hbm, coef_v), (src_hbm, src_v), (att_hbm, att_v),
             (wgt_hbm, wgt_v), (tiles_hbm, tiles_v), (seg_hbm, seg_ref), (cnt_hbm, cnt_ref))
        )
    ]
    for copy in loads:
        copy.start()

    def strided(ref, row):
        return ref[pl.ds(row, nb, stride=ROWS_MSG), :]

    def put(ref, row, value):
        ref[pl.ds(row, nb, stride=ROWS_MSG), :] = value

    def group_start(k):
        return pl.multiple_of(jnp.bitwise_xor(my_group, k) * (GROUP * ROWS_MSG), GROUP * ROWS_MSG)

    def strided_group(ref, row, k):
        return ref[pl.ds(group_start(k) + row, GROUP, stride=ROWS_MSG), :]

    def put_group(ref, row, k, value):
        ref[pl.ds(group_start(k) + row, GROUP, stride=ROWS_MSG), :] = value

    def block(q, first, rows):
        return pl.ds(pl.multiple_of(q * ROWS_MSG, ROWS_MSG) + first, rows)

    def send_group(src, dst, phase, k, first, rows):
        for j in within:
            step = k * GROUP + j
            if step == 0:
                continue
            q = jnp.bitwise_xor(me, step)
            pltpu.make_async_remote_copy(
                src_ref=src.at[block(q, first, rows)], dst_ref=dst.at[block(me, first, rows)],
                send_sem=send_sem.at[phase], recv_sem=recv_sem.at[phase, k],
                device_id=(z, q), device_id_type=pl.DeviceIdType.MESH,
            ).start()

    def keep(src, dst):
        dst[block(me, 0, ROWS_MSG), :] = src[block(me, 0, ROWS_MSG), :]

    def await_bytes(ref, rows, sem):
        view = ref.at[pl.ds(0, rows)]
        pltpu.make_async_copy(view, view, sem).wait()

    def await_group(ref, phase, k, rows):
        await_bytes(ref, (GROUP - (k == 0)) * rows, recv_sem.at[phase, k])

    bins, lane = iota((nb, LANES), 0), iota((nb, LANES), 1)
    loads[0].wait()
    src_shift = src_dev.bit_length() - 1
    idx = idx_v[...]
    owner = idx >> src_shift
    mine = [jnp.broadcast_to(owner[t : t + 1], (nb, LANES)) == bins for t in range(td)]
    ones = [m.astype(F32) for m in mine]
    i0, i1 = iota((LANES, 2 * LANES), 0), iota((LANES, 2 * LANES), 1)
    tri = ((i0 < i1) | (i1 >= LANES)).astype(F32).astype(BF16)
    counts = jnp.dot(
        jnp.concatenate(ones, axis=0).astype(BF16), tri, preferred_element_type=F32
    )
    offset = jnp.zeros((nb, LANES), F32)
    slot_id = iota((LANES, LANES), 0)
    spots, origin = [], []
    lane_f = lane.astype(F32)
    for t in range(td):
        here = counts[t * nb : (t + 1) * nb]
        rank = jnp.sum(jnp.where(mine[t], here[:, :LANES] + offset, 0.0), axis=0, keepdims=True)
        rank = rank.astype(I32)
        offset = offset + here[:, LANES:]
        rank_v[t : t + 1, :] = rank
        spots.append((jnp.broadcast_to(rank, (LANES, LANES)) == slot_id).astype(F32).astype(BF16))
        origin.append(jnp.concatenate([ones[t] * (t + 1.0), ones[t] * lane_f], axis=0).astype(BF16))
    found = lax.dot_general(
        jnp.concatenate(origin, axis=1), jnp.concatenate(spots, axis=1), NT,
        preferred_element_type=F32,
    ).astype(I32)
    inv_v[...] = found

    def to_slots(rows):
        tile, col = inv_v[:nb, :], inv_v[nb:, :]
        out = jnp.zeros((nb, LANES), F32)
        for t in range(td):
            out = jnp.where(tile == t + 1, lanes_of(rows[t : t + 1], col), out)
        return out

    loads[1].wait()
    for k in range(params):
        put(s1, k, to_slots(coef_v[k]))
    put(s1, params, to_slots((idx & (src_dev - 1)).astype(F32)))

    loads[6].wait()
    seg_shift = seg_dev.bit_length() - 1
    owner_t = [seg_ref[t] >> seg_shift for t in range(td)]
    local_t = [seg_ref[t] & (seg_dev - 1) for t in range(td)]
    rank_t = []
    for t in range(td):
        r = jnp.int32(0)
        for before in range(t):
            r = r + (owner_t[before] == owner_t[t]).astype(I32)
        rank_t.append(r)
    wanted = jnp.zeros((nb, LANES), I32)
    for t in range(td):
        hit = (bins == owner_t[t]) & (lane == rank_t[t])
        wanted = jnp.where(hit, local_t[t] + 1, wanted)
    put(s1, params + 1, wanted.astype(F32))

    asked_rows = params + 2
    pl.semaphore_wait(barrier, n_tm + n_sky - 2)
    for k in across:
        send_group(s1, r1, 0, k, 0, asked_rows)
    keep(s1, r1)

    loads[5].wait()

    @pl.loop(0, td)
    def _(t):
        rows = pl.ds(pl.multiple_of(t * LANES, LANES), LANES)
        hi, lo = halves(tiles_v[t])
        thi[rows, :] = hi
        tlo[rows, :] = lo
        hi, lo = halves(tiles_v[t].T)
        thi_t[:, rows] = hi
        tlo_t[:, rows] = lo

    for copy in (loads[2], loads[3], loads[4], loads[7]):
        copy.wait()
    att_pair = jnp.concatenate(halves(att_v[...]), axis=1)
    obs_t, obs_row = iota((td, LANES), 0), iota((td, LANES), 1)
    count = jnp.zeros((td, LANES), I32)
    for t in range(td):
        count = jnp.where(obs_t == t, cnt_ref[t], count)
    live = obs_row < count

    answer_rows = 1 + SLOT_T * half
    seg_id = iota((GROUP, seg_dev), 1) + 1
    for k in reversed(across):
        await_group(r1, 0, k, asked_rows)
        asked = strided_group(r1, params, k).astype(I32)
        chunk, col = asked >> 7, asked & (LANES - 1)
        picked = [jnp.zeros((GROUP, LANES), F32) for _ in range(params)]
        for h in range(chunks):
            here = chunk == h
            for p in range(params):
                row = src_v[p : p + 1, h * LANES : (h + 1) * LANES]
                picked[p] = jnp.where(here, lanes_of(row, col), picked[p])
        total = jnp.zeros((GROUP, LANES), F32)
        for p in range(params):
            total = total + strided_group(r1, p, k) * picked[p]
        put_group(s2, 0, k, total)
        segs = strided_group(r1, params + 1, k).astype(I32)
        pick = jnp.concatenate(
            [
                jnp.broadcast_to(segs[:, r : r + 1], (GROUP, seg_dev)) == seg_id
                for r in range(SLOT_T)
            ],
            axis=0,
        ).astype(F32).astype(BF16)
        both = jnp.dot(pick, att_pair, preferred_element_type=F32)
        rows = both[:, :cols] + both[:, cols:]
        for r in range(SLOT_T):
            for c in range(half):
                put_group(
                    s2, 1 + r * half + c, k,
                    rows[r * GROUP : (r + 1) * GROUP, c * LANES : (c + 1) * LANES],
                )
        send_group(s2, r2, 1, k, 0, answer_rows)
    keep(s2, r2)

    asked = strided(r1, params).astype(I32)
    chunk, col = asked >> 7, asked & (LANES - 1)
    for p in range(nb):
        low_v[:, p * LANES : (p + 1) * LANES] = (
            jnp.broadcast_to(col[p : p + 1], (LANES, LANES)) == slot_id
        ).astype(F32).astype(BF16)
    segs = strided(r1, params + 1).astype(I32)
    choice = jnp.concatenate(
        [
            jnp.broadcast_to(segs[:, r : r + 1], (nb, LANES)) == iota((nb, LANES), 1) + 1
            for r in range(SLOT_T)
        ],
        axis=0,
    ).astype(F32)
    choice = choice.T[:seg_dev].astype(BF16)

    rank = rank_v[...]
    source = jnp.zeros((td, LANES), F32)
    for k in reversed(across):
        await_group(r2, 1, k, answer_rows)
        answers = strided_group(r2, 0, k)
        first = jnp.bitwise_xor(my_group, k) * GROUP
        for w in range(GROUP):
            source = jnp.where(owner == first + w, lanes_of(answers[w : w + 1], rank), source)
    for t in range(td):
        for c in range(half):
            dir_v[t : t + 1, c * LANES : (c + 1) * LANES] = r2[
                pl.ds(owner_t[t] * ROWS_MSG + 1 + rank_t[t] * half + c, 1), :
            ]
    dir_hi, dir_lo = halves(dir_v[...])
    first = jnp.dot(
        jnp.concatenate([dir_hi, dir_lo], axis=0), thi_t[...], preferred_element_type=F32
    )
    second = jnp.dot(dir_hi, tlo_t[...], preferred_element_type=F32)
    sums = first[:td] + first[td:] + second
    part = jnp.zeros((td, LANES), F32)
    for t in range(td):
        part = jnp.where(obs_t == t, sums[:, t * LANES : (t + 1) * LANES], part)
    projected = jnp.where(live, part + source, 0.0)
    proj_o[...] = projected
    weighted = wgt_v[...] * projected
    curvature = jnp.sum(projected * weighted, axis=0, keepdims=True)

    w_hi, w_lo = halves(weighted)
    w_hi, w_lo = w_hi.astype(F32), w_lo.astype(F32)
    slots = iota((SLOT_T * nb, LANES), 0)
    left = []
    for t in range(td):
        here = slots == rank_t[t] * nb + owner_t[t]
        left.append(
            jnp.concatenate(
                [
                    jnp.where(here, jnp.broadcast_to(w[t : t + 1], slots.shape), 0.0)
                    for w in (w_hi, w_lo)
                ],
                axis=0,
            ).astype(BF16)
        )
    left = jnp.concatenate(left, axis=1)
    n_slots = SLOT_T * nb
    grad = jnp.dot(left, thi[...], preferred_element_type=F32)
    grad = (
        grad[:n_slots]
        + grad[n_slots:]
        + jnp.dot(left[:n_slots], tlo[...], preferred_element_type=F32)
    )
    for r in range(SLOT_T):
        for c in range(half):
            put(
                s3, r * half + c,
                grad[r * nb : (r + 1) * nb, c * LANES : (c + 1) * LANES],
            )
    curv_row = SLOT_T * half
    put(s3, curv_row, jnp.broadcast_to(curvature, (nb, LANES)))
    for k in across:
        send_group(s3, r3, 2, k, 0, curv_row + 1)
    weight_row = curv_row + 1
    put(s3, weight_row, to_slots(weighted))
    for k in across:
        send_group(s3, r3, 3, k, weight_row, 1)
    keep(s3, r3)
    for k in across:
        await_group(r3, 2, k, curv_row + 1)

    zrows = seg_dev * half + 1
    pitch = rz.shape[0] // n_sky

    def zblock(q):
        return pl.ds(pl.multiple_of(q * pitch, 8), zrows)

    rows = jnp.concatenate(
        [
            jnp.concatenate([strided(r3, r * half + c) for c in range(half)], axis=1)
            for r in range(SLOT_T)
        ],
        axis=0,
    )
    both = jnp.dot(
        choice, jnp.concatenate(halves(rows), axis=1), preferred_element_type=F32
    )
    owned = both[:, :cols] + both[:, cols:]
    for c in range(half):
        sz[c * seg_dev : (c + 1) * seg_dev, :] = owned[:, c * LANES : (c + 1) * LANES]
    sz[zrows - 1 : zrows, :] = jnp.sum(strided(r3, curv_row), axis=0, keepdims=True)

    for i in sorted(range(1, n_sky), key=lambda i: -min(i, n_sky - i)):
        q = lax.rem(z + i, n_sky)
        pltpu.make_async_remote_copy(
            src_ref=sz.at[pl.ds(0, zrows)], dst_ref=rz.at[zblock(z)],
            send_sem=zsend_sem.at[0], recv_sem=zrecv_sem.at[0],
            device_id=(q, me), device_id_type=pl.DeviceIdType.MESH,
        ).start()

    rz[zblock(z), :] = sz[0:zrows, :]

    for k in across:
        await_group(r3, 3, k, 1)
    back = strided(r3, weight_row)
    chunk_id = iota((chunks, LANES), 0)
    terms = []
    for k in range(params):
        hi, lo = halves(strided(r1, k) * back)
        terms.append((hi.astype(F32), lo.astype(F32)))
    grid = []
    for p in range(nb):
        here = jnp.broadcast_to(chunk[p : p + 1], chunk_id.shape) == chunk_id
        grid.append(
            jnp.concatenate(
                [
                    jnp.where(here, jnp.broadcast_to(terms[k][i][p : p + 1], here.shape), 0.0)
                    for i in range(2)
                    for k in range(params)
                ],
                axis=0,
            ).astype(BF16)
        )
    both = lax.dot_general(
        jnp.concatenate(grid, axis=1), low_v[...], NT, preferred_element_type=F32
    )
    rows = params * chunks
    spread = both[:rows] + both[rows:]
    for k in range(params):
        for h in range(chunks):
            src_o[k : k + 1, h * LANES : (h + 1) * LANES] = spread[
                k * chunks + h : k * chunks + h + 1
            ]

    for k, (ref, rows) in enumerate(
        ((s1, asked_rows), (s2, answer_rows), (s3, curv_row + 1), (s3, 1))
    ):
        await_bytes(ref, (n_tm - 1) * rows, send_sem.at[k])
    await_bytes(rz, (n_sky - 1) * zrows, zrecv_sem.at[0])
    summed = rz[0:zrows, :]
    for q in range(1, n_sky):
        summed = summed + rz[q * pitch : q * pitch + zrows, :]
    sums_o[0:zrows, :] = summed
    await_bytes(rz, (n_sky - 1) * zrows, zsend_sem.at[0])


def hand_over(proj, sums, src, proj_o, att_o, src_o, curv_o):
    seg_dev, cols = att_o.shape
    half = cols // LANES
    proj_o[...] = proj[...]
    src_o[...] = src[...]
    for c in range(half):
        att_o[:, c * LANES : (c + 1) * LANES] = sums[c * seg_dev : (c + 1) * seg_dev, :]
    curv_o[0] = jnp.sum(sums[seg_dev * half : seg_dev * half + 1, :])


def per_device(n_sky, n_tm, tiles, tile_seg, tile_count, src_index, src_coef, obs_weight, att_dir, src_dir):
    td, rows, cols = tiles.shape
    params, src_dev = src_dir.shape
    seg_dev = att_dir.shape[0]
    groups = n_tm // GROUP
    msg = pltpu.VMEM((n_tm * ROWS_MSG, LANES), F32)
    pitch = seg_dev * (cols // LANES) + 8
    vmem, smem, hbm = (
        pl.BlockSpec(memory_space=s) for s in (pltpu.VMEM, pltpu.SMEM, pl.ANY)
    )
    projected, sums, src_normal = pl.pallas_call(
        functools.partial(kernel, n_sky, n_tm),
        out_shape=(
            jax.ShapeDtypeStruct((td, rows), F32),
            jax.ShapeDtypeStruct((pitch, LANES), F32),
            jax.ShapeDtypeStruct((params, src_dev), F32),
        ),
        in_specs=[hbm, hbm, hbm, hbm, hbm, hbm, hbm, hbm],
        out_specs=(vmem, vmem, vmem),
        scratch_shapes=[
            pltpu.SMEM((td,), I32),
            pltpu.SMEM((td,), I32),
            pltpu.VMEM((td, rows, cols), F32),
            pltpu.VMEM((td, rows), I32),
            pltpu.VMEM((params, td, rows), F32),
            pltpu.VMEM((td, rows), F32),
            pltpu.VMEM((seg_dev, cols), F32),
            pltpu.VMEM((params, src_dev), F32),
            pltpu.VMEM((td * rows, cols), BF16),
            pltpu.VMEM((td * rows, cols), BF16),
            pltpu.VMEM((cols, td * rows), BF16),
            pltpu.VMEM((cols, td * rows), BF16),
            pltpu.VMEM((LANES, n_tm * LANES), BF16),
            pltpu.VMEM((td, cols), F32),
            pltpu.VMEM((td, rows), I32),
            pltpu.VMEM((2 * n_tm, LANES), I32),
            msg, msg, msg, msg, msg, msg,
            pltpu.VMEM((pitch, LANES), F32),
            pltpu.VMEM((n_sky * pitch, LANES), F32),
            pltpu.SemaphoreType.DMA((8,)),
            pltpu.SemaphoreType.DMA((4,)),
            pltpu.SemaphoreType.DMA((4, groups)),
            pltpu.SemaphoreType.DMA((1,)),
            pltpu.SemaphoreType.DMA((1,)),
        ],
        compiler_params=pltpu.CompilerParams(
            collective_id=0, has_side_effects=True, vmem_limit_bytes=SCOPED
        ),
    )(
        *[
            pltpu.with_memory_space_constraint(x, pltpu.HBM)
            for x in (
                tile_seg, tile_count, tiles, src_index, src_coef, obs_weight, att_dir, src_dir,
            )
        ]
    )
    projected, att_normal, src_normal, curvature = pl.pallas_call(
        hand_over,
        out_shape=(
            jax.ShapeDtypeStruct((td, rows), F32),
            jax.ShapeDtypeStruct((seg_dev, cols), F32),
            jax.ShapeDtypeStruct((params, src_dev), F32),
            jax.ShapeDtypeStruct((1,), F32),
        ),
        in_specs=[vmem, vmem, vmem],
        out_specs=(vmem, vmem, vmem, smem),
        compiler_params=pltpu.CompilerParams(vmem_limit_bytes=SCOPED),
    )(projected, sums, src_normal)
    return projected, att_normal, src_normal, curvature.reshape(())


def solution(mesh):
    placed = (
        P(("sky", "tm"), None, None),
        P(("sky", "tm")),
        P(("sky", "tm")),
        P(("sky", "tm"), None),
        P(None, ("sky", "tm"), None),
        P(("sky", "tm"), None),
        P("tm", None),
        P(None, ("sky", "tm")),
    )
    return jax.shard_map(
        functools.partial(per_device, mesh.shape["sky"], mesh.shape["tm"]),
        mesh=mesh,
        in_specs=placed,
        out_specs=(P(("sky", "tm"), None), P("tm", None), P(None, ("sky", "tm")), P()),
        check_vma=False,
    )
```

```python
import functools

import jax
import jax.numpy as jnp
from jax import lax
from jax.experimental import pallas as pl
from jax.experimental.pallas import tpu as pltpu
from jax.sharding import PartitionSpec as P

LANES = 128
ROWS_MSG = 8
GROUP = 8
PACKED = 16
SCOPED = 44 << 20
SLOT_T = 2
F32, BF16, I32 = jnp.float32, jnp.bfloat16, jnp.int32
NT = (((1,), (1,)), ((), ()))


def halves(x):
    hi = x.astype(BF16)
    return hi, (x - hi.astype(F32)).astype(BF16)


def iota(shape, dim):
    return lax.broadcasted_iota(I32, shape, dim)


def lanes_of(row, index):
    return jnp.take_along_axis(jnp.broadcast_to(row, index.shape), index, axis=1)


def hops(step, extents):
    total = 0
    for n in reversed(extents):
        part = step % n
        step //= n
        total += min(part, n - part)
    return total


def kernel(
    n_sky, n_tm,
    seg_hbm, cnt_hbm, tiles_hbm, idx_hbm, coef_hbm, wgt_hbm, att_hbm, src_hbm,
    proj_o, sums_o, src_o,
    seg_ref, cnt_ref, tiles_v, idx_v, coef_v, wgt_v, att_v, src_v, thi, tlo, thi_t, tlo_t, slot_v, low_v, dir_v, rank_v, inv_v,
    s1, r1, s2, r2, s3, r3, sz, rz,
    in_sem, send_sem, recv_sem, zsend_sem, zrecv_sem,
):
    params, td, _ = coef_v.shape
    seg_dev, cols = att_v.shape
    src_dev = src_v.shape[1]
    nb = n_tm
    groups = n_tm // GROUP
    chunks = src_dev // LANES
    half = cols // LANES
    me, z = lax.axis_index("tm"), lax.axis_index("sky")
    my_group = me // GROUP
    across = sorted(range(groups), key=lambda k: -min(k, groups - k))
    within = sorted(range(GROUP), key=lambda k: -hops(k, (4, 2)))

    barrier = pltpu.get_barrier_semaphore()

    for k in across:
        for j in within:
            if k or j:
                q = jnp.bitwise_xor(me, k * GROUP + j)
                pl.semaphore_signal(barrier, 1, device_id=(z, q))

    @pl.loop(1, n_sky)
    def _(i):
        pl.semaphore_signal(barrier, 1, device_id=(lax.rem(z + i, n_sky), me))

    loads = [
        pltpu.make_async_copy(a, b, in_sem.at[i])
        for i, (a, b) in enumerate(
            ((idx_hbm, idx_v), (coef_hbm, coef_v), (src_hbm, src_v), (att_hbm, att_v),
             (wgt_hbm, wgt_v), (tiles_hbm, tiles_v), (seg_hbm, seg_ref), (cnt_hbm, cnt_ref))
        )
    ]
    for copy in loads:
        copy.start()

    def strided(ref, row):
        return ref[pl.ds(row, nb, stride=ROWS_MSG), :]

    def put(ref, row, value):
        ref[pl.ds(row, nb, stride=ROWS_MSG), :] = value

    def group_start(k):
        return pl.multiple_of(jnp.bitwise_xor(my_group, k) * (GROUP * ROWS_MSG), GROUP * ROWS_MSG)

    def strided_group(ref, row, k):
        return ref[pl.ds(group_start(k) + row, GROUP, stride=ROWS_MSG), :]

    def put_group(ref, row, k, value):
        ref[pl.ds(group_start(k) + row, GROUP, stride=ROWS_MSG), :] = value

    def block(q, first, rows):
        return pl.ds(pl.multiple_of(q * ROWS_MSG, ROWS_MSG) + first, rows)

    def send_group(src, dst, phase, k, first, rows):
        for j in within:
            step = k * GROUP + j
            if step == 0:
                continue
            q = jnp.bitwise_xor(me, step)
            pltpu.make_async_remote_copy(
                src_ref=src.at[block(q, first, rows)], dst_ref=dst.at[block(me, first, rows)],
                send_sem=send_sem.at[phase], recv_sem=recv_sem.at[phase, k],
                device_id=(z, q), device_id_type=pl.DeviceIdType.MESH,
            ).start()

    def keep(src, dst):
        dst[block(me, 0, ROWS_MSG), :] = src[block(me, 0, ROWS_MSG), :]

    def await_bytes(ref, rows, sem):
        view = ref.at[pl.ds(0, rows)]
        pltpu.make_async_copy(view, view, sem).wait()

    def await_group(ref, phase, k, rows):
        await_bytes(ref, (GROUP - (k == 0)) * rows, recv_sem.at[phase, k])

    bins, lane = iota((nb, LANES), 0), iota((nb, LANES), 1)
    loads[0].wait()
    src_shift = src_dev.bit_length() - 1
    idx = idx_v[...]
    owner = idx >> src_shift
    mine = [jnp.broadcast_to(owner[t : t + 1], (nb, LANES)) == bins for t in range(td)]
    ones = [m.astype(F32) for m in mine]
    i0, i1 = iota((LANES, 2 * LANES), 0), iota((LANES, 2 * LANES), 1)
    tri = ((i0 < i1) | (i1 >= LANES)).astype(F32).astype(BF16)
    counts = jnp.dot(
        jnp.concatenate(ones, axis=0).astype(BF16), tri, preferred_element_type=F32
    )
    offset = jnp.zeros((nb, LANES), F32)
    slot_id = iota((LANES, LANES), 0)
    spots, origin = [], []
    lane_f = lane.astype(F32)
    for t in range(td):
        here = counts[t * nb : (t + 1) * nb]
        rank = jnp.sum(jnp.where(mine[t], here[:, :LANES] + offset, 0.0), axis=0, keepdims=True)
        rank = rank.astype(I32)
        offset = offset + here[:, LANES:]
        rank_v[t : t + 1, :] = rank
        spots.append((jnp.broadcast_to(rank, (LANES, LANES)) == slot_id).astype(F32).astype(BF16))
        origin.append(jnp.concatenate([ones[t] * (t + 1.0), ones[t] * lane_f], axis=0).astype(BF16))
    found = lax.dot_general(
        jnp.concatenate(origin, axis=1), jnp.concatenate(spots, axis=1), NT,
        preferred_element_type=F32,
    ).astype(I32)
    inv_v[...] = found

    def to_slots(rows):
        tile, col = inv_v[:nb, :], inv_v[nb:, :]
        out = jnp.zeros((nb, LANES), F32)
        for t in range(td):
            out = jnp.where(tile == t + 1, lanes_of(rows[t : t + 1], col), out)
        return out

    loads[1].wait()
    for k in range(params):
        put(s1, k, to_slots(coef_v[k]))
    put(s1, params, to_slots((idx & (src_dev - 1)).astype(F32)))

    loads[6].wait()
    seg_shift = seg_dev.bit_length() - 1
    owner_t = [seg_ref[t] >> seg_shift for t in range(td)]
    local_t = [seg_ref[t] & (seg_dev - 1) for t in range(td)]
    rank_t = []
    for t in range(td):
        r = jnp.int32(0)
        for before in range(t):
            r = r + (owner_t[before] == owner_t[t]).astype(I32)
        rank_t.append(r)
    wanted = jnp.zeros((nb, LANES), I32)
    for t in range(td):
        hit = (bins == owner_t[t]) & (lane == rank_t[t])
        wanted = jnp.where(hit, local_t[t] + 1, wanted)
    put(s1, params + 1, wanted.astype(F32))

    asked_rows = params + 2
    pl.semaphore_wait(barrier, n_tm + n_sky - 2)
    for k in across:
        send_group(s1, r1, 0, k, 0, asked_rows)
    keep(s1, r1)

    n_slots = SLOT_T * nb
    slots = iota((n_slots, LANES), 0)
    for t in range(td):
        slot_v[:, t * LANES : (t + 1) * LANES] = (
            (slots == rank_t[t] * nb + owner_t[t]).astype(F32).astype(BF16)
        )
    loads[5].wait()

    @pl.loop(0, td)
    def _(t):
        rows = pl.ds(pl.multiple_of(t * LANES, LANES), LANES)
        hi, lo = halves(tiles_v[t])
        thi[rows, :] = hi
        tlo[rows, :] = lo
        hi, lo = halves(tiles_v[t].T)
        thi_t[:, rows] = hi
        tlo_t[:, rows] = lo

    for copy in (loads[2], loads[3], loads[4], loads[7]):
        copy.wait()
    obs_t, obs_row = iota((td, LANES), 0), iota((td, LANES), 1)
    count = jnp.zeros((td, LANES), I32)
    for t in range(td):
        count = jnp.where(obs_t == t, cnt_ref[t], count)
    live = obs_row < count

    answer_rows = 1 + SLOT_T * half
    @pl.loop(0, groups)
    def _(i):
        k = jnp.bitwise_xor(i, i >> 1)

        @pl.when(i == 0)
        def _():
            await_group(r1, 0, 0, asked_rows)

        @pl.when(i > 0)
        def _():
            await_bytes(r1, GROUP * asked_rows, recv_sem.at[0, k])

        asked = strided_group(r1, params, k).astype(I32)
        chunk, col = asked >> 7, asked & (LANES - 1)
        picked = [jnp.zeros((GROUP, LANES), F32) for _ in range(params)]
        for h in range(chunks):
            here = chunk == h
            for p in range(params):
                row = src_v[p : p + 1, h * LANES : (h + 1) * LANES]
                picked[p] = jnp.where(here, lanes_of(row, col), picked[p])
        total = jnp.zeros((GROUP, LANES), F32)
        for p in range(params):
            total = total + strided_group(r1, p, k) * picked[p]
        put_group(s2, 0, k, total)
        segs = strided_group(r1, params + 1, k).astype(I32)
        for r in range(SLOT_T):
            seg = jnp.broadcast_to(segs[:, r : r + 1], (GROUP, LANES))
            rows = [jnp.zeros((GROUP, LANES), F32) for _ in range(half)]
            for n in range(seg_dev):
                here = seg == n + 1
                for c in range(half):
                    row = att_v[n : n + 1, c * LANES : (c + 1) * LANES]
                    rows[c] = jnp.where(here, jnp.broadcast_to(row, here.shape), rows[c])
            for c in range(half):
                put_group(s2, 1 + r * half + c, k, rows[c])
        for j in within:

            @pl.when((i > 0) | (j > 0))
            def _(j=j):
                q = jnp.bitwise_xor(me, k * GROUP + j)
                pltpu.make_async_remote_copy(
                    src_ref=s2.at[block(q, 0, answer_rows)],
                    dst_ref=r2.at[block(me, 0, answer_rows)],
                    send_sem=send_sem.at[1], recv_sem=recv_sem.at[1, k],
                    device_id=(z, q), device_id_type=pl.DeviceIdType.MESH,
                ).start()

    keep(s2, r2)

    asked = strided(r1, params).astype(I32)
    chunk, col = asked >> 7, asked & (LANES - 1)
    for p in range(nb):
        low_v[:, p * LANES : (p + 1) * LANES] = (
            jnp.broadcast_to(col[p : p + 1], (LANES, LANES)) == slot_id
        ).astype(F32).astype(BF16)
    segs = strided(r1, params + 1).astype(I32)
    choice = jnp.concatenate(
        [
            jnp.broadcast_to(segs[:, r : r + 1], (nb, LANES)) == iota((nb, LANES), 1) + 1
            for r in range(SLOT_T)
        ],
        axis=0,
    ).astype(F32)
    choice = choice.T[:seg_dev].astype(BF16)

    rank = rank_v[...]
    source = jnp.zeros((td, LANES), F32)
    for k in reversed(across):
        await_group(r2, 1, k, answer_rows)
        answers = strided_group(r2, 0, k)
        first = jnp.bitwise_xor(my_group, k) * GROUP
        for w in range(GROUP):
            source = jnp.where(owner == first + w, lanes_of(answers[w : w + 1], rank), source)
    for t in range(td):
        for c in range(half):
            dir_v[t : t + 1, c * LANES : (c + 1) * LANES] = r2[
                pl.ds(owner_t[t] * ROWS_MSG + 1 + rank_t[t] * half + c, 1), :
            ]
    dir_hi, dir_lo = halves(dir_v[...])
    first = jnp.dot(
        jnp.concatenate([dir_hi, dir_lo], axis=0), thi_t[...], preferred_element_type=F32
    )
    second = jnp.dot(dir_hi, tlo_t[...], preferred_element_type=F32)
    sums = first[:td] + first[td:] + second
    part = jnp.zeros((td, LANES), F32)
    for t in range(td):
        part = jnp.where(obs_t == t, sums[:, t * LANES : (t + 1) * LANES], part)
    projected = jnp.where(live, part + source, 0.0)
    proj_o[...] = projected
    weighted = wgt_v[...] * projected
    curvature = jnp.sum(projected * weighted, axis=0, keepdims=True)

    left = []
    for w in halves(weighted):
        w = w.astype(F32)
        spread = [
            jnp.broadcast_to(w[t : t + 1], (PACKED, LANES)).astype(BF16) for t in range(td)
        ]
        row = jnp.concatenate(spread, axis=1)
        left.append(jnp.concatenate([row] * (n_slots // PACKED), axis=0) * slot_v[...])
    left = jnp.concatenate(left, axis=0)
    grad = jnp.dot(left, thi[...], preferred_element_type=F32)
    grad = (
        grad[:n_slots]
        + grad[n_slots:]
        + jnp.dot(left[:n_slots], tlo[...], preferred_element_type=F32)
    )
    for r in range(SLOT_T):
        for c in range(half):
            put(
                s3, r * half + c,
                grad[r * nb : (r + 1) * nb, c * LANES : (c + 1) * LANES],
            )
    curv_row = SLOT_T * half
    put(s3, curv_row, jnp.broadcast_to(curvature, (nb, LANES)))
    for k in across:
        send_group(s3, r3, 2, k, 0, curv_row + 1)
    weight_row = curv_row + 1
    put(s3, weight_row, to_slots(weighted))
    for k in across:
        send_group(s3, r3, 3, k, weight_row, 1)
    keep(s3, r3)
    for k in across:
        await_group(r3, 2, k, curv_row + 1)

    zrows = seg_dev * half + 1
    pitch = rz.shape[0] // n_sky

    def zblock(q):
        return pl.ds(pl.multiple_of(q * pitch, 8), zrows)

    rows = jnp.concatenate(
        [
            jnp.concatenate([strided(r3, r * half + c) for c in range(half)], axis=1)
            for r in range(SLOT_T)
        ],
        axis=0,
    )
    both = jnp.dot(
        choice, jnp.concatenate(halves(rows), axis=1), preferred_element_type=F32
    )
    owned = both[:, :cols] + both[:, cols:]
    for c in range(half):
        sz[c * seg_dev : (c + 1) * seg_dev, :] = owned[:, c * LANES : (c + 1) * LANES]
    sz[zrows - 1 : zrows, :] = jnp.sum(strided(r3, curv_row), axis=0, keepdims=True)

    for i in sorted(range(1, n_sky), key=lambda i: -min(i, n_sky - i)):
        q = lax.rem(z + i, n_sky)
        pltpu.make_async_remote_copy(
            src_ref=sz.at[pl.ds(0, zrows)], dst_ref=rz.at[zblock(z)],
            send_sem=zsend_sem.at[0], recv_sem=zrecv_sem.at[0],
            device_id=(q, me), device_id_type=pl.DeviceIdType.MESH,
        ).start()

    rz[zblock(z), :] = sz[0:zrows, :]

    for k in across:
        await_group(r3, 3, k, 1)
    back = strided(r3, weight_row)
    chunk_id = iota((chunks, LANES), 0)
    terms = []
    for k in range(params):
        hi, lo = halves(strided(r1, k) * back)
        terms.append((hi.astype(F32), lo.astype(F32)))
    grid = []
    for p in range(nb):
        here = jnp.broadcast_to(chunk[p : p + 1], chunk_id.shape) == chunk_id
        grid.append(
            jnp.concatenate(
                [
                    jnp.where(here, jnp.broadcast_to(terms[k][i][p : p + 1], here.shape), 0.0)
                    for i in range(2)
                    for k in range(params)
                ],
                axis=0,
            ).astype(BF16)
        )
    both = lax.dot_general(
        jnp.concatenate(grid, axis=1), low_v[...], NT, preferred_element_type=F32
    )
    rows = params * chunks
    spread = both[:rows] + both[rows:]
    for k in range(params):
        for h in range(chunks):
            src_o[k : k + 1, h * LANES : (h + 1) * LANES] = spread[
                k * chunks + h : k * chunks + h + 1
            ]

    for k, (ref, rows) in enumerate(
        ((s1, asked_rows), (s2, answer_rows), (s3, curv_row + 1), (s3, 1))
    ):
        await_bytes(ref, (n_tm - 1) * rows, send_sem.at[k])
    await_bytes(rz, (n_sky - 1) * zrows, zrecv_sem.at[0])
    summed = rz[0:zrows, :]
    for q in range(1, n_sky):
        summed = summed + rz[q * pitch : q * pitch + zrows, :]
    sums_o[0:zrows, :] = summed
    await_bytes(rz, (n_sky - 1) * zrows, zsend_sem.at[0])


def hand_over(proj, sums, src, proj_o, att_o, src_o, curv_o):
    seg_dev, cols = att_o.shape
    half = cols // LANES
    proj_o[...] = proj[...]
    src_o[...] = src[...]
    for c in range(half):
        att_o[:, c * LANES : (c + 1) * LANES] = sums[c * seg_dev : (c + 1) * seg_dev, :]
    curv_o[0] = jnp.sum(sums[seg_dev * half : seg_dev * half + 1, :])


def per_device(n_sky, n_tm, tiles, tile_seg, tile_count, src_index, src_coef, obs_weight, att_dir, src_dir):
    td, rows, cols = tiles.shape
    params, src_dev = src_dir.shape
    seg_dev = att_dir.shape[0]
    groups = n_tm // GROUP
    msg = pltpu.VMEM((n_tm * ROWS_MSG, LANES), F32)
    pitch = seg_dev * (cols // LANES) + 8
    vmem, smem, hbm = (
        pl.BlockSpec(memory_space=s) for s in (pltpu.VMEM, pltpu.SMEM, pl.ANY)
    )
    projected, sums, src_normal = pl.pallas_call(
        functools.partial(kernel, n_sky, n_tm),
        out_shape=(
            jax.ShapeDtypeStruct((td, rows), F32),
            jax.ShapeDtypeStruct((pitch, LANES), F32),
            jax.ShapeDtypeStruct((params, src_dev), F32),
        ),
        in_specs=[hbm, hbm, hbm, hbm, hbm, hbm, hbm, hbm],
        out_specs=(vmem, vmem, vmem),
        scratch_shapes=[
            pltpu.SMEM((td,), I32),
            pltpu.SMEM((td,), I32),
            pltpu.VMEM((td, rows, cols), F32),
            pltpu.VMEM((td, rows), I32),
            pltpu.VMEM((params, td, rows), F32),
            pltpu.VMEM((td, rows), F32),
            pltpu.VMEM((seg_dev, cols), F32),
            pltpu.VMEM((params, src_dev), F32),
            pltpu.VMEM((td * rows, cols), BF16),
            pltpu.VMEM((td * rows, cols), BF16),
            pltpu.VMEM((cols, td * rows), BF16),
            pltpu.VMEM((cols, td * rows), BF16),
            pltpu.VMEM((SLOT_T * n_tm, td * rows), BF16),
            pltpu.VMEM((LANES, n_tm * LANES), BF16),
            pltpu.VMEM((td, cols), F32),
            pltpu.VMEM((td, rows), I32),
            pltpu.VMEM((2 * n_tm, LANES), I32),
            msg, msg, msg, msg, msg, msg,
            pltpu.VMEM((pitch, LANES), F32),
            pltpu.VMEM((n_sky * pitch, LANES), F32),
            pltpu.SemaphoreType.DMA((8,)),
            pltpu.SemaphoreType.DMA((4,)),
            pltpu.SemaphoreType.DMA((4, groups)),
            pltpu.SemaphoreType.DMA((1,)),
            pltpu.SemaphoreType.DMA((1,)),
        ],
        compiler_params=pltpu.CompilerParams(
            collective_id=0, has_side_effects=True, vmem_limit_bytes=SCOPED
        ),
    )(
        *[
            pltpu.with_memory_space_constraint(x, pltpu.HBM)
            for x in (
                tile_seg, tile_count, tiles, src_index, src_coef, obs_weight, att_dir, src_dir,
            )
        ]
    )
    projected, att_normal, src_normal, curvature = pl.pallas_call(
        hand_over,
        out_shape=(
            jax.ShapeDtypeStruct((td, rows), F32),
            jax.ShapeDtypeStruct((seg_dev, cols), F32),
            jax.ShapeDtypeStruct((params, src_dev), F32),
            jax.ShapeDtypeStruct((1,), F32),
        ),
        in_specs=[vmem, vmem, vmem],
        out_specs=(vmem, vmem, vmem, smem),
        compiler_params=pltpu.CompilerParams(vmem_limit_bytes=SCOPED),
    )(projected, sums, src_normal)
    return projected, att_normal, src_normal, curvature.reshape(())


def solution(mesh):
    placed = (
        P(("sky", "tm"), None, None),
        P(("sky", "tm")),
        P(("sky", "tm")),
        P(("sky", "tm"), None),
        P(None, ("sky", "tm"), None),
        P(("sky", "tm"), None),
        P("tm", None),
        P(None, ("sky", "tm")),
    )
    return jax.shard_map(
        functools.partial(per_device, mesh.shape["sky"], mesh.shape["tm"]),
        mesh=mesh,
        in_specs=placed,
        out_specs=(P(("sky", "tm"), None), P("tm", None), P(None, ("sky", "tm")), P()),
        check_vma=False,
    )
```

```python
import functools

import jax
import jax.numpy as jnp
from jax import lax
from jax.experimental import pallas as pl
from jax.experimental.pallas import tpu as pltpu
from jax.sharding import PartitionSpec as P

LANES = 128
ROWS_MSG = 8
GROUP = 8
PACKED = 16
SCOPED = 44 << 20
SLOT_T = 2
F32, BF16, I32 = jnp.float32, jnp.bfloat16, jnp.int32
NT = (((1,), (1,)), ((), ()))


def halves(x):
    hi = x.astype(BF16)
    return hi, (x - hi.astype(F32)).astype(BF16)


def iota(shape, dim):
    return lax.broadcasted_iota(I32, shape, dim)


def lanes_of(row, index):
    return jnp.take_along_axis(jnp.broadcast_to(row, index.shape), index, axis=1)


def hops(step, extents):
    total = 0
    for n in reversed(extents):
        part = step % n
        step //= n
        total += min(part, n - part)
    return total


def kernel(
    n_sky, n_tm,
    seg_hbm, cnt_hbm, tiles_hbm, idx_hbm, coef_hbm, wgt_hbm, att_hbm, src_hbm,
    proj_o, sums_o, src_o,
    seg_ref, cnt_ref, tiles_v, idx_v, coef_v, wgt_v, att_v, src_v, thi, tlo, thi_t, tlo_t, slot_v, low_v, dir_v, rank_v, inv_v,
    s1, r1, s2, r2, s3, r3, sz, rz,
    in_sem, send_sem, recv_sem, zsend_sem, zrecv_sem,
):
    params, td, _ = coef_v.shape
    seg_dev, cols = att_v.shape
    src_dev = src_v.shape[1]
    nb = n_tm
    groups = n_tm // GROUP
    chunks = src_dev // LANES
    half = cols // LANES
    me, z = lax.axis_index("tm"), lax.axis_index("sky")
    my_group = me // GROUP
    across = sorted(range(groups), key=lambda k: -min(k, groups - k))
    within = sorted(range(GROUP), key=lambda k: -hops(k, (4, 2)))

    barrier = pltpu.get_barrier_semaphore()

    for k in across:
        for j in within:
            if k or j:
                q = jnp.bitwise_xor(me, k * GROUP + j)
                pl.semaphore_signal(barrier, 1, device_id=(z, q))

    @pl.loop(1, n_sky)
    def _(i):
        pl.semaphore_signal(barrier, 1, device_id=(lax.rem(z + i, n_sky), me))

    loads = [
        pltpu.make_async_copy(a, b, in_sem.at[i])
        for i, (a, b) in enumerate(
            ((idx_hbm, idx_v), (coef_hbm, coef_v), (src_hbm, src_v), (att_hbm, att_v),
             (wgt_hbm, wgt_v), (tiles_hbm, tiles_v), (seg_hbm, seg_ref), (cnt_hbm, cnt_ref))
        )
    ]
    for copy in loads:
        copy.start()

    def strided(ref, row):
        return ref[pl.ds(row, nb, stride=ROWS_MSG), :]

    def put(ref, row, value):
        ref[pl.ds(row, nb, stride=ROWS_MSG), :] = value

    def group_start(k):
        return pl.multiple_of(jnp.bitwise_xor(my_group, k) * (GROUP * ROWS_MSG), GROUP * ROWS_MSG)

    def strided_group(ref, row, k):
        return ref[pl.ds(group_start(k) + row, GROUP, stride=ROWS_MSG), :]

    def put_group(ref, row, k, value):
        ref[pl.ds(group_start(k) + row, GROUP, stride=ROWS_MSG), :] = value

    def block(q, first, rows):
        return pl.ds(pl.multiple_of(q * ROWS_MSG, ROWS_MSG) + first, rows)

    def send_group(src, dst, phase, k, first, rows):
        for j in within:
            step = k * GROUP + j
            if step == 0:
                continue
            q = jnp.bitwise_xor(me, step)
            pltpu.make_async_remote_copy(
                src_ref=src.at[block(q, first, rows)], dst_ref=dst.at[block(me, first, rows)],
                send_sem=send_sem.at[phase], recv_sem=recv_sem.at[phase, k],
                device_id=(z, q), device_id_type=pl.DeviceIdType.MESH,
            ).start()

    def keep(src, dst):
        dst[block(me, 0, ROWS_MSG), :] = src[block(me, 0, ROWS_MSG), :]

    def await_bytes(ref, rows, sem):
        view = ref.at[pl.ds(0, rows)]
        pltpu.make_async_copy(view, view, sem).wait()

    def await_group(ref, phase, k, rows):
        await_bytes(ref, (GROUP - (k == 0)) * rows, recv_sem.at[phase, k])

    loads[7].wait()
    obs_t, obs_row = iota((td, LANES), 0), iota((td, LANES), 1)
    count = jnp.zeros((td, LANES), I32)
    for t in range(td):
        count = jnp.where(obs_t == t, cnt_ref[t], count)
    live = obs_row < count
    bins, lane = iota((nb, LANES), 0), iota((nb, LANES), 1)
    loads[0].wait()
    src_shift = src_dev.bit_length() - 1
    idx = idx_v[...]
    owner = jnp.where(live, idx >> src_shift, -1)
    mine = [jnp.broadcast_to(owner[t : t + 1], (nb, LANES)) == bins for t in range(td)]
    ones = [m.astype(F32) for m in mine]
    i0, i1 = iota((LANES, 2 * LANES), 0), iota((LANES, 2 * LANES), 1)
    tri = ((i0 < i1) | (i1 >= LANES)).astype(F32).astype(BF16)
    counts = jnp.dot(
        jnp.concatenate(ones, axis=0).astype(BF16), tri, preferred_element_type=F32
    )
    offset = jnp.zeros((nb, LANES), F32)
    slot_id = iota((LANES, LANES), 0)
    spots, origin = [], []
    lane_f = lane.astype(F32)
    for t in range(td):
        here = counts[t * nb : (t + 1) * nb]
        rank = jnp.sum(jnp.where(mine[t], here[:, :LANES] + offset, 0.0), axis=0, keepdims=True)
        rank = rank.astype(I32)
        offset = offset + here[:, LANES:]
        rank_v[t : t + 1, :] = rank
        spots.append((jnp.broadcast_to(rank, (LANES, LANES)) == slot_id).astype(F32).astype(BF16))
        origin.append(jnp.concatenate([ones[t] * (t + 1.0), ones[t] * lane_f], axis=0).astype(BF16))
    found = lax.dot_general(
        jnp.concatenate(origin, axis=1), jnp.concatenate(spots, axis=1), NT,
        preferred_element_type=F32,
    ).astype(I32)
    inv_v[...] = found

    def to_slots(rows):
        tile, col = inv_v[:nb, :], inv_v[nb:, :]
        out = jnp.zeros((nb, LANES), F32)
        for t in range(td):
            out = jnp.where(tile == t + 1, lanes_of(rows[t : t + 1], col), out)
        return out

    loads[1].wait()
    for k in range(params):
        put(s1, k, to_slots(coef_v[k]))
    put(s1, params, to_slots((idx & (src_dev - 1)).astype(F32)))

    loads[6].wait()
    seg_shift = seg_dev.bit_length() - 1
    owner_t = [seg_ref[t] >> seg_shift for t in range(td)]
    local_t = [seg_ref[t] & (seg_dev - 1) for t in range(td)]
    rank_t = []
    for t in range(td):
        r = jnp.int32(0)
        for before in range(t):
            r = r + (owner_t[before] == owner_t[t]).astype(I32)
        rank_t.append(r)
    wanted = jnp.zeros((nb, LANES), I32)
    for t in range(td):
        hit = (bins == owner_t[t]) & (lane == rank_t[t])
        wanted = jnp.where(hit, local_t[t] + 1, wanted)
    put(s1, params + 1, wanted.astype(F32))

    asked_rows = params + 2
    pl.semaphore_wait(barrier, n_tm + n_sky - 2)
    for k in across:
        send_group(s1, r1, 0, k, 0, asked_rows)
    keep(s1, r1)

    n_slots = SLOT_T * nb
    slots = iota((n_slots, LANES), 0)
    for t in range(td):
        slot_v[:, t * LANES : (t + 1) * LANES] = (
            (slots == rank_t[t] * nb + owner_t[t]).astype(F32).astype(BF16)
        )
    loads[5].wait()

    @pl.loop(0, td)
    def _(t):
        rows = pl.ds(pl.multiple_of(t * LANES, LANES), LANES)
        hi, lo = halves(tiles_v[t])
        thi[rows, :] = hi
        tlo[rows, :] = lo
        hi, lo = halves(tiles_v[t].T)
        thi_t[:, rows] = hi
        tlo_t[:, rows] = lo

    for copy in (loads[2], loads[3], loads[4]):
        copy.wait()

    answer_rows = 1 + SLOT_T * half
    @pl.loop(0, groups)
    def _(i):
        k = jnp.bitwise_xor(i, i >> 1)

        @pl.when(i == 0)
        def _():
            await_group(r1, 0, 0, asked_rows)

        @pl.when(i > 0)
        def _():
            await_bytes(r1, GROUP * asked_rows, recv_sem.at[0, k])

        asked = strided_group(r1, params, k).astype(I32)
        chunk, col = asked >> 7, asked & (LANES - 1)
        picked = [jnp.zeros((GROUP, LANES), F32) for _ in range(params)]
        for h in range(chunks):
            here = chunk == h
            for p in range(params):
                row = src_v[p : p + 1, h * LANES : (h + 1) * LANES]
                picked[p] = jnp.where(here, lanes_of(row, col), picked[p])
        total = jnp.zeros((GROUP, LANES), F32)
        for p in range(params):
            total = total + strided_group(r1, p, k) * picked[p]
        put_group(s2, 0, k, total)
        segs = strided_group(r1, params + 1, k).astype(I32)
        for r in range(SLOT_T):
            seg = jnp.broadcast_to(segs[:, r : r + 1], (GROUP, LANES))
            rows = [jnp.zeros((GROUP, LANES), F32) for _ in range(half)]
            for n in range(seg_dev):
                here = seg == n + 1
                for c in range(half):
                    row = att_v[n : n + 1, c * LANES : (c + 1) * LANES]
                    rows[c] = jnp.where(here, jnp.broadcast_to(row, here.shape), rows[c])
            for c in range(half):
                put_group(s2, 1 + r * half + c, k, rows[c])
        for j in within:

            @pl.when((i > 0) | (j > 0))
            def _(j=j):
                q = jnp.bitwise_xor(me, k * GROUP + j)
                pltpu.make_async_remote_copy(
                    src_ref=s2.at[block(q, 0, answer_rows)],
                    dst_ref=r2.at[block(me, 0, answer_rows)],
                    send_sem=send_sem.at[1], recv_sem=recv_sem.at[1, k],
                    device_id=(z, q), device_id_type=pl.DeviceIdType.MESH,
                ).start()

    keep(s2, r2)

    asked = strided(r1, params).astype(I32)
    chunk, col = asked >> 7, asked & (LANES - 1)
    for p in range(nb):
        low_v[:, p * LANES : (p + 1) * LANES] = (
            jnp.broadcast_to(col[p : p + 1], (LANES, LANES)) == slot_id
        ).astype(F32).astype(BF16)
    segs = strided(r1, params + 1).astype(I32)
    choice = jnp.concatenate(
        [
            jnp.broadcast_to(segs[:, r : r + 1], (nb, LANES)) == iota((nb, LANES), 1) + 1
            for r in range(SLOT_T)
        ],
        axis=0,
    ).astype(F32)
    choice = choice.T[:seg_dev].astype(BF16)

    rank = rank_v[...]
    source = jnp.zeros((td, LANES), F32)
    for k in reversed(across):
        await_group(r2, 1, k, answer_rows)
        answers = strided_group(r2, 0, k)
        first = jnp.bitwise_xor(my_group, k) * GROUP
        for w in range(GROUP):
            source = jnp.where(owner == first + w, lanes_of(answers[w : w + 1], rank), source)
    for t in range(td):
        for c in range(half):
            dir_v[t : t + 1, c * LANES : (c + 1) * LANES] = r2[
                pl.ds(owner_t[t] * ROWS_MSG + 1 + rank_t[t] * half + c, 1), :
            ]
    dir_hi, dir_lo = halves(dir_v[...])
    first = jnp.dot(
        jnp.concatenate([dir_hi, dir_lo], axis=0), thi_t[...], preferred_element_type=F32
    )
    second = jnp.dot(dir_hi, tlo_t[...], preferred_element_type=F32)
    sums = first[:td] + first[td:] + second
    part = jnp.zeros((td, LANES), F32)
    for t in range(td):
        part = jnp.where(obs_t == t, sums[:, t * LANES : (t + 1) * LANES], part)
    projected = jnp.where(live, part + source, 0.0)
    proj_o[...] = projected
    weighted = wgt_v[...] * projected
    curvature = jnp.sum(projected * weighted, axis=0, keepdims=True)

    left = []
    for w in halves(weighted):
        w = w.astype(F32)
        spread = [
            jnp.broadcast_to(w[t : t + 1], (PACKED, LANES)).astype(BF16) for t in range(td)
        ]
        row = jnp.concatenate(spread, axis=1)
        left.append(jnp.concatenate([row] * (n_slots // PACKED), axis=0) * slot_v[...])
    left = jnp.concatenate(left, axis=0)
    grad = jnp.dot(left, thi[...], preferred_element_type=F32)
    grad = (
        grad[:n_slots]
        + grad[n_slots:]
        + jnp.dot(left[:n_slots], tlo[...], preferred_element_type=F32)
    )
    for r in range(SLOT_T):
        for c in range(half):
            put(
                s3, r * half + c,
                grad[r * nb : (r + 1) * nb, c * LANES : (c + 1) * LANES],
            )
    curv_row = SLOT_T * half
    put(s3, curv_row, jnp.broadcast_to(curvature, (nb, LANES)))
    for k in across:
        send_group(s3, r3, 2, k, 0, curv_row + 1)
    weight_row = curv_row + 1
    put(s3, weight_row, to_slots(weighted))
    for k in across:
        send_group(s3, r3, 3, k, weight_row, 1)
    keep(s3, r3)
    for k in across:
        await_group(r3, 2, k, curv_row + 1)

    zrows = seg_dev * half + 1
    pitch = rz.shape[0] // n_sky

    def zblock(q):
        return pl.ds(pl.multiple_of(q * pitch, 8), zrows)

    rows = jnp.concatenate(
        [
            jnp.concatenate([strided(r3, r * half + c) for c in range(half)], axis=1)
            for r in range(SLOT_T)
        ],
        axis=0,
    )
    both = jnp.dot(
        choice, jnp.concatenate(halves(rows), axis=1), preferred_element_type=F32
    )
    owned = both[:, :cols] + both[:, cols:]
    for c in range(half):
        sz[c * seg_dev : (c + 1) * seg_dev, :] = owned[:, c * LANES : (c + 1) * LANES]
    sz[zrows - 1 : zrows, :] = jnp.sum(strided(r3, curv_row), axis=0, keepdims=True)

    for i in sorted(range(1, n_sky), key=lambda i: -min(i, n_sky - i)):
        q = lax.rem(z + i, n_sky)
        pltpu.make_async_remote_copy(
            src_ref=sz.at[pl.ds(0, zrows)], dst_ref=rz.at[zblock(z)],
            send_sem=zsend_sem.at[0], recv_sem=zrecv_sem.at[0],
            device_id=(q, me), device_id_type=pl.DeviceIdType.MESH,
        ).start()

    rz[zblock(z), :] = sz[0:zrows, :]

    for k in across:
        await_group(r3, 3, k, 1)
    back = strided(r3, weight_row)
    chunk_id = iota((chunks, LANES), 0)
    terms = []
    for k in range(params):
        hi, lo = halves(strided(r1, k) * back)
        terms.append((hi.astype(F32), lo.astype(F32)))
    grid = []
    for p in range(nb):
        here = jnp.broadcast_to(chunk[p : p + 1], chunk_id.shape) == chunk_id
        grid.append(
            jnp.concatenate(
                [
                    jnp.where(here, jnp.broadcast_to(terms[k][i][p : p + 1], here.shape), 0.0)
                    for i in range(2)
                    for k in range(params)
                ],
                axis=0,
            ).astype(BF16)
        )
    both = lax.dot_general(
        jnp.concatenate(grid, axis=1), low_v[...], NT, preferred_element_type=F32
    )
    rows = params * chunks
    spread = both[:rows] + both[rows:]
    for k in range(params):
        for h in range(chunks):
            src_o[k : k + 1, h * LANES : (h + 1) * LANES] = spread[
                k * chunks + h : k * chunks + h + 1
            ]

    for k, (ref, rows) in enumerate(
        ((s1, asked_rows), (s2, answer_rows), (s3, curv_row + 1), (s3, 1))
    ):
        await_bytes(ref, (n_tm - 1) * rows, send_sem.at[k])
    await_bytes(rz, (n_sky - 1) * zrows, zrecv_sem.at[0])
    summed = rz[0:zrows, :]
    for q in range(1, n_sky):
        summed = summed + rz[q * pitch : q * pitch + zrows, :]
    sums_o[0:zrows, :] = summed
    await_bytes(rz, (n_sky - 1) * zrows, zsend_sem.at[0])


def hand_over(proj, sums, src, proj_o, att_o, src_o, curv_o):
    seg_dev, cols = att_o.shape
    half = cols // LANES
    proj_o[...] = proj[...]
    src_o[...] = src[...]
    for c in range(half):
        att_o[:, c * LANES : (c + 1) * LANES] = sums[c * seg_dev : (c + 1) * seg_dev, :]
    curv_o[0] = jnp.sum(sums[seg_dev * half : seg_dev * half + 1, :])


def per_device(n_sky, n_tm, tiles, tile_seg, tile_count, src_index, src_coef, obs_weight, att_dir, src_dir):
    td, rows, cols = tiles.shape
    params, src_dev = src_dir.shape
    seg_dev = att_dir.shape[0]
    groups = n_tm // GROUP
    msg = pltpu.VMEM((n_tm * ROWS_MSG, LANES), F32)
    pitch = seg_dev * (cols // LANES) + 8
    vmem, smem, hbm = (
        pl.BlockSpec(memory_space=s) for s in (pltpu.VMEM, pltpu.SMEM, pl.ANY)
    )
    projected, sums, src_normal = pl.pallas_call(
        functools.partial(kernel, n_sky, n_tm),
        out_shape=(
            jax.ShapeDtypeStruct((td, rows), F32),
            jax.ShapeDtypeStruct((pitch, LANES), F32),
            jax.ShapeDtypeStruct((params, src_dev), F32),
        ),
        in_specs=[hbm, hbm, hbm, hbm, hbm, hbm, hbm, hbm],
        out_specs=(vmem, vmem, vmem),
        scratch_shapes=[
            pltpu.SMEM((td,), I32),
            pltpu.SMEM((td,), I32),
            pltpu.VMEM((td, rows, cols), F32),
            pltpu.VMEM((td, rows), I32),
            pltpu.VMEM((params, td, rows), F32),
            pltpu.VMEM((td, rows), F32),
            pltpu.VMEM((seg_dev, cols), F32),
            pltpu.VMEM((params, src_dev), F32),
            pltpu.VMEM((td * rows, cols), BF16),
            pltpu.VMEM((td * rows, cols), BF16),
            pltpu.VMEM((cols, td * rows), BF16),
            pltpu.VMEM((cols, td * rows), BF16),
            pltpu.VMEM((SLOT_T * n_tm, td * rows), BF16),
            pltpu.VMEM((LANES, n_tm * LANES), BF16),
            pltpu.VMEM((td, cols), F32),
            pltpu.VMEM((td, rows), I32),
            pltpu.VMEM((2 * n_tm, LANES), I32),
            msg, msg, msg, msg, msg, msg,
            pltpu.VMEM((pitch, LANES), F32),
            pltpu.VMEM((n_sky * pitch, LANES), F32),
            pltpu.SemaphoreType.DMA((8,)),
            pltpu.SemaphoreType.DMA((4,)),
            pltpu.SemaphoreType.DMA((4, groups)),
            pltpu.SemaphoreType.DMA((1,)),
            pltpu.SemaphoreType.DMA((1,)),
        ],
        compiler_params=pltpu.CompilerParams(
            collective_id=0, has_side_effects=True, vmem_limit_bytes=SCOPED
        ),
    )(
        *[
            pltpu.with_memory_space_constraint(x, pltpu.HBM)
            for x in (
                tile_seg, tile_count, tiles, src_index, src_coef, obs_weight, att_dir, src_dir,
            )
        ]
    )
    projected, att_normal, src_normal, curvature = pl.pallas_call(
        hand_over,
        out_shape=(
            jax.ShapeDtypeStruct((td, rows), F32),
            jax.ShapeDtypeStruct((seg_dev, cols), F32),
            jax.ShapeDtypeStruct((params, src_dev), F32),
            jax.ShapeDtypeStruct((1,), F32),
        ),
        in_specs=[vmem, vmem, vmem],
        out_specs=(vmem, vmem, vmem, smem),
        compiler_params=pltpu.CompilerParams(vmem_limit_bytes=SCOPED),
    )(projected, sums, src_normal)
    return projected, att_normal, src_normal, curvature.reshape(())


def solution(mesh):
    placed = (
        P(("sky", "tm"), None, None),
        P(("sky", "tm")),
        P(("sky", "tm")),
        P(("sky", "tm"), None),
        P(None, ("sky", "tm"), None),
        P(("sky", "tm"), None),
        P("tm", None),
        P(None, ("sky", "tm")),
    )
    return jax.shard_map(
        functools.partial(per_device, mesh.shape["sky"], mesh.shape["tm"]),
        mesh=mesh,
        in_specs=placed,
        out_specs=(P(("sky", "tm"), None), P("tm", None), P(None, ("sky", "tm")), P()),
        check_vma=False,
    )
```

```python
import functools

import jax
import jax.numpy as jnp
from jax import lax
from jax.experimental import pallas as pl
from jax.experimental.pallas import tpu as pltpu
from jax.sharding import PartitionSpec as P

LANES = 128
ROWS_MSG = 8
GROUP = 8
PACKED = 16
SCOPED = 44 << 20
SLOT_T = 2
F32, BF16, I32 = jnp.float32, jnp.bfloat16, jnp.int32
NT = (((1,), (1,)), ((), ()))


def halves(x):
    hi = x.astype(BF16)
    return hi, (x - hi.astype(F32)).astype(BF16)


def iota(shape, dim):
    return lax.broadcasted_iota(I32, shape, dim)


def lanes_of(row, index):
    return jnp.take_along_axis(jnp.broadcast_to(row, index.shape), index, axis=1)


def hops(step, extents):
    total = 0
    for n in reversed(extents):
        part = step % n
        step //= n
        total += min(part, n - part)
    return total


def kernel(
    n_sky, n_tm,
    seg_hbm, cnt_hbm, tiles_hbm, idx_hbm, coef_hbm, wgt_hbm, att_hbm, src_hbm,
    proj_o, sums_o, src_o,
    seg_ref, cnt_ref, tiles_v, idx_v, coef_v, wgt_v, att_v, src_v, thi, tlo, thi_t, tlo_t, slot_v, low_v, dir_v, rank_v, inv_v,
    s1, r1, s2, r2, s3, r3, sz, rz,
    in_sem, send_sem, recv_sem, zsend_sem, zrecv_sem,
):
    params, td, _ = coef_v.shape
    seg_dev, cols = att_v.shape
    src_dev = src_v.shape[1]
    nb = n_tm
    groups = n_tm // GROUP
    chunks = src_dev // LANES
    half = cols // LANES
    me, z = lax.axis_index("tm"), lax.axis_index("sky")
    my_group = me // GROUP
    across = sorted(range(groups), key=lambda k: -min(k, groups - k))
    within = sorted(range(GROUP), key=lambda k: -hops(k, (4, 2)))

    barrier = pltpu.get_barrier_semaphore()

    for k in across:
        for j in within:
            if k or j:
                q = jnp.bitwise_xor(me, k * GROUP + j)
                pl.semaphore_signal(barrier, 1, device_id=(z, q))

    @pl.loop(1, n_sky)
    def _(i):
        pl.semaphore_signal(barrier, 1, device_id=(lax.rem(z + i, n_sky), me))

    loads = [
        pltpu.make_async_copy(a, b, in_sem.at[i])
        for i, (a, b) in enumerate(
            ((idx_hbm, idx_v), (coef_hbm, coef_v), (src_hbm, src_v), (att_hbm, att_v),
             (wgt_hbm, wgt_v), (tiles_hbm, tiles_v), (seg_hbm, seg_ref), (cnt_hbm, cnt_ref))
        )
    ]
    for i in (7, 0, 6, 1, 2, 3, 4, 5):
        loads[i].start()

    def strided(ref, row):
        return ref[pl.ds(row, nb, stride=ROWS_MSG), :]

    def put(ref, row, value):
        ref[pl.ds(row, nb, stride=ROWS_MSG), :] = value

    def group_start(k):
        return pl.multiple_of(jnp.bitwise_xor(my_group, k) * (GROUP * ROWS_MSG), GROUP * ROWS_MSG)

    def strided_group(ref, row, k):
        return ref[pl.ds(group_start(k) + row, GROUP, stride=ROWS_MSG), :]

    def put_group(ref, row, k, value):
        ref[pl.ds(group_start(k) + row, GROUP, stride=ROWS_MSG), :] = value

    def block(q, first, rows):
        return pl.ds(pl.multiple_of(q * ROWS_MSG, ROWS_MSG) + first, rows)

    def send_group(src, dst, phase, k, first, rows):
        for j in within:
            step = k * GROUP + j
            if step == 0:
                continue
            q = jnp.bitwise_xor(me, step)
            pltpu.make_async_remote_copy(
                src_ref=src.at[block(q, first, rows)], dst_ref=dst.at[block(me, first, rows)],
                send_sem=send_sem.at[phase], recv_sem=recv_sem.at[phase, k],
                device_id=(z, q), device_id_type=pl.DeviceIdType.MESH,
            ).start()

    def keep(src, dst):
        dst[block(me, 0, ROWS_MSG), :] = src[block(me, 0, ROWS_MSG), :]

    def await_bytes(ref, rows, sem):
        view = ref.at[pl.ds(0, rows)]
        pltpu.make_async_copy(view, view, sem).wait()

    def await_group(ref, phase, k, rows):
        await_bytes(ref, (GROUP - (k == 0)) * rows, recv_sem.at[phase, k])

    loads[7].wait()
    obs_t, obs_row = iota((td, LANES), 0), iota((td, LANES), 1)
    count = jnp.zeros((td, LANES), I32)
    for t in range(td):
        count = jnp.where(obs_t == t, cnt_ref[t], count)
    live = obs_row < count
    bins, lane = iota((nb, LANES), 0), iota((nb, LANES), 1)
    loads[0].wait()
    src_shift = src_dev.bit_length() - 1
    idx = idx_v[...]
    owner = jnp.where(live, idx >> src_shift, -1)
    mine = [jnp.broadcast_to(owner[t : t + 1], (nb, LANES)) == bins for t in range(td)]
    ones = [m.astype(F32) for m in mine]
    i0, i1 = iota((LANES, 2 * LANES), 0), iota((LANES, 2 * LANES), 1)
    tri = ((i0 < i1) | (i1 >= LANES)).astype(F32).astype(BF16)
    counts = jnp.dot(
        jnp.concatenate(ones, axis=0).astype(BF16), tri, preferred_element_type=F32
    )
    offset = jnp.zeros((nb, LANES), F32)
    slot_id = iota((LANES, LANES), 0)
    spots, origin = [], []
    lane_f = lane.astype(F32)
    for t in range(td):
        here = counts[t * nb : (t + 1) * nb]
        rank = jnp.sum(jnp.where(mine[t], here[:, :LANES] + offset, 0.0), axis=0, keepdims=True)
        rank = rank.astype(I32)
        offset = offset + here[:, LANES:]
        rank_v[t : t + 1, :] = rank
        spots.append((jnp.broadcast_to(rank, (LANES, LANES)) == slot_id).astype(F32).astype(BF16))
        origin.append(jnp.concatenate([ones[t] * (t + 1.0), ones[t] * lane_f], axis=0).astype(BF16))
    found = lax.dot_general(
        jnp.concatenate(origin, axis=1), jnp.concatenate(spots, axis=1), NT,
        preferred_element_type=F32,
    ).astype(I32)
    inv_v[...] = found

    def to_slots(rows):
        tile, col = inv_v[:nb, :], inv_v[nb:, :]
        out = jnp.zeros((nb, LANES), F32)
        for t in range(td):
            out = jnp.where(tile == t + 1, lanes_of(rows[t : t + 1], col), out)
        return out

    loads[1].wait()
    for k in range(params):
        put(s1, k, to_slots(coef_v[k]))
    put(s1, params, to_slots((idx & (src_dev - 1)).astype(F32)))

    loads[6].wait()
    seg_shift = seg_dev.bit_length() - 1
    owner_t = [seg_ref[t] >> seg_shift for t in range(td)]
    local_t = [seg_ref[t] & (seg_dev - 1) for t in range(td)]
    rank_t = []
    for t in range(td):
        r = jnp.int32(0)
        for before in range(t):
            r = r + (owner_t[before] == owner_t[t]).astype(I32)
        rank_t.append(r)
    wanted = jnp.zeros((nb, LANES), I32)
    for t in range(td):
        hit = (bins == owner_t[t]) & (lane == rank_t[t])
        wanted = jnp.where(hit, local_t[t] + 1, wanted)
    put(s1, params + 1, wanted.astype(F32))

    asked_rows = params + 2
    pl.semaphore_wait(barrier, n_tm + n_sky - 2)
    for k in across:
        send_group(s1, r1, 0, k, 0, asked_rows)
    keep(s1, r1)

    n_slots = SLOT_T * nb
    slots = iota((n_slots, LANES), 0)
    for t in range(td):
        slot_v[:, t * LANES : (t + 1) * LANES] = (
            (slots == rank_t[t] * nb + owner_t[t]).astype(F32).astype(BF16)
        )
    loads[5].wait()

    @pl.loop(0, td)
    def _(t):
        rows = pl.ds(pl.multiple_of(t * LANES, LANES), LANES)
        hi, lo = halves(tiles_v[t])
        thi[rows, :] = hi
        tlo[rows, :] = lo
        hi, lo = halves(tiles_v[t].T)
        thi_t[:, rows] = hi
        tlo_t[:, rows] = lo

    for copy in (loads[2], loads[3], loads[4]):
        copy.wait()

    answer_rows = 1 + SLOT_T * half
    @pl.loop(0, groups)
    def _(i):
        k = jnp.bitwise_xor(i, i >> 1)

        @pl.when(i == 0)
        def _():
            await_group(r1, 0, 0, asked_rows)

        @pl.when(i > 0)
        def _():
            await_bytes(r1, GROUP * asked_rows, recv_sem.at[0, k])

        asked = strided_group(r1, params, k).astype(I32)
        chunk, col = asked >> 7, asked & (LANES - 1)
        picked = [jnp.zeros((GROUP, LANES), F32) for _ in range(params)]
        for h in range(chunks):
            here = chunk == h
            for p in range(params):
                row = src_v[p : p + 1, h * LANES : (h + 1) * LANES]
                picked[p] = jnp.where(here, lanes_of(row, col), picked[p])
        total = jnp.zeros((GROUP, LANES), F32)
        for p in range(params):
            total = total + strided_group(r1, p, k) * picked[p]
        put_group(s2, 0, k, total)
        segs = strided_group(r1, params + 1, k).astype(I32)
        for r in range(SLOT_T):
            seg = jnp.broadcast_to(segs[:, r : r + 1], (GROUP, LANES))
            rows = [jnp.zeros((GROUP, LANES), F32) for _ in range(half)]
            for n in range(seg_dev):
                here = seg == n + 1
                for c in range(half):
                    row = att_v[n : n + 1, c * LANES : (c + 1) * LANES]
                    rows[c] = jnp.where(here, jnp.broadcast_to(row, here.shape), rows[c])
            for c in range(half):
                put_group(s2, 1 + r * half + c, k, rows[c])
        for j in within:

            @pl.when((i > 0) | (j > 0))
            def _(j=j):
                q = jnp.bitwise_xor(me, k * GROUP + j)
                pltpu.make_async_remote_copy(
                    src_ref=s2.at[block(q, 0, answer_rows)],
                    dst_ref=r2.at[block(me, 0, answer_rows)],
                    send_sem=send_sem.at[1], recv_sem=recv_sem.at[1, k],
                    device_id=(z, q), device_id_type=pl.DeviceIdType.MESH,
                ).start()

    keep(s2, r2)

    asked = strided(r1, params).astype(I32)
    chunk, col = asked >> 7, asked & (LANES - 1)
    for p in range(nb):
        low_v[:, p * LANES : (p + 1) * LANES] = (
            jnp.broadcast_to(col[p : p + 1], (LANES, LANES)) == slot_id
        ).astype(F32).astype(BF16)
    segs = strided(r1, params + 1).astype(I32)
    choice = jnp.concatenate(
        [
            jnp.broadcast_to(segs[:, r : r + 1], (nb, LANES)) == iota((nb, LANES), 1) + 1
            for r in range(SLOT_T)
        ],
        axis=0,
    ).astype(F32)
    choice = choice.T[:seg_dev].astype(BF16)

    rank = rank_v[...]
    source = jnp.zeros((td, LANES), F32)
    for k in reversed(across):
        await_group(r2, 1, k, answer_rows)
        answers = strided_group(r2, 0, k)
        first = jnp.bitwise_xor(my_group, k) * GROUP
        for w in range(GROUP):
            source = jnp.where(owner == first + w, lanes_of(answers[w : w + 1], rank), source)
    for t in range(td):
        for c in range(half):
            dir_v[t : t + 1, c * LANES : (c + 1) * LANES] = r2[
                pl.ds(owner_t[t] * ROWS_MSG + 1 + rank_t[t] * half + c, 1), :
            ]
    dir_hi, dir_lo = halves(dir_v[...])
    first = jnp.dot(
        jnp.concatenate([dir_hi, dir_lo], axis=0), thi_t[...], preferred_element_type=F32
    )
    second = jnp.dot(dir_hi, tlo_t[...], preferred_element_type=F32)
    sums = first[:td] + first[td:] + second
    part = jnp.zeros((td, LANES), F32)
    for t in range(td):
        part = jnp.where(obs_t == t, sums[:, t * LANES : (t + 1) * LANES], part)
    projected = jnp.where(live, part + source, 0.0)
    proj_o[...] = projected
    weighted = wgt_v[...] * projected
    curvature = jnp.sum(projected * weighted, axis=0, keepdims=True)

    left = []
    for w in halves(weighted):
        w = w.astype(F32)
        spread = [
            jnp.broadcast_to(w[t : t + 1], (PACKED, LANES)).astype(BF16) for t in range(td)
        ]
        row = jnp.concatenate(spread, axis=1)
        left.append(jnp.concatenate([row] * (n_slots // PACKED), axis=0) * slot_v[...])
    left = jnp.concatenate(left, axis=0)
    grad = jnp.dot(left, thi[...], preferred_element_type=F32)
    grad = (
        grad[:n_slots]
        + grad[n_slots:]
        + jnp.dot(left[:n_slots], tlo[...], preferred_element_type=F32)
    )
    for r in range(SLOT_T):
        for c in range(half):
            put(
                s3, r * half + c,
                grad[r * nb : (r + 1) * nb, c * LANES : (c + 1) * LANES],
            )
    curv_row = SLOT_T * half
    put(s3, curv_row, jnp.broadcast_to(curvature, (nb, LANES)))
    for k in across:
        send_group(s3, r3, 2, k, 0, curv_row + 1)
    weight_row = curv_row + 1
    put(s3, weight_row, to_slots(weighted))
    for k in across:
        send_group(s3, r3, 3, k, weight_row, 1)
    keep(s3, r3)
    for k in across:
        await_group(r3, 2, k, curv_row + 1)

    zrows = seg_dev * half + 1
    pitch = rz.shape[0] // n_sky

    def zblock(q):
        return pl.ds(pl.multiple_of(q * pitch, 8), zrows)

    rows = jnp.concatenate(
        [
            jnp.concatenate([strided(r3, r * half + c) for c in range(half)], axis=1)
            for r in range(SLOT_T)
        ],
        axis=0,
    )
    both = jnp.dot(
        choice, jnp.concatenate(halves(rows), axis=1), preferred_element_type=F32
    )
    owned = both[:, :cols] + both[:, cols:]
    for c in range(half):
        sz[c * seg_dev : (c + 1) * seg_dev, :] = owned[:, c * LANES : (c + 1) * LANES]
    sz[zrows - 1 : zrows, :] = jnp.sum(strided(r3, curv_row), axis=0, keepdims=True)

    for i in sorted(range(1, n_sky), key=lambda i: -min(i, n_sky - i)):
        q = lax.rem(z + i, n_sky)
        pltpu.make_async_remote_copy(
            src_ref=sz.at[pl.ds(0, zrows)], dst_ref=rz.at[zblock(z)],
            send_sem=zsend_sem.at[0], recv_sem=zrecv_sem.at[0],
            device_id=(q, me), device_id_type=pl.DeviceIdType.MESH,
        ).start()

    rz[zblock(z), :] = sz[0:zrows, :]

    for k in across:
        await_group(r3, 3, k, 1)
    back = strided(r3, weight_row)
    chunk_id = iota((chunks, LANES), 0)
    terms = []
    for k in range(params):
        hi, lo = halves(strided(r1, k) * back)
        terms.append((hi.astype(F32), lo.astype(F32)))
    grid = []
    for p in range(nb):
        here = jnp.broadcast_to(chunk[p : p + 1], chunk_id.shape) == chunk_id
        grid.append(
            jnp.concatenate(
                [
                    jnp.where(here, jnp.broadcast_to(terms[k][i][p : p + 1], here.shape), 0.0)
                    for i in range(2)
                    for k in range(params)
                ],
                axis=0,
            ).astype(BF16)
        )
    both = lax.dot_general(
        jnp.concatenate(grid, axis=1), low_v[...], NT, preferred_element_type=F32
    )
    rows = params * chunks
    spread = both[:rows] + both[rows:]
    for k in range(params):
        for h in range(chunks):
            src_o[k : k + 1, h * LANES : (h + 1) * LANES] = spread[
                k * chunks + h : k * chunks + h + 1
            ]

    for k, (ref, rows) in enumerate(
        ((s1, asked_rows), (s2, answer_rows), (s3, curv_row + 1), (s3, 1))
    ):
        await_bytes(ref, (n_tm - 1) * rows, send_sem.at[k])
    await_bytes(rz, (n_sky - 1) * zrows, zrecv_sem.at[0])
    summed = rz[0:zrows, :]
    for q in range(1, n_sky):
        summed = summed + rz[q * pitch : q * pitch + zrows, :]
    sums_o[0:zrows, :] = summed
    await_bytes(rz, (n_sky - 1) * zrows, zsend_sem.at[0])


def hand_over(proj, sums, src, proj_o, att_o, src_o, curv_o):
    seg_dev, cols = att_o.shape
    half = cols // LANES
    proj_o[...] = proj[...]
    src_o[...] = src[...]
    for c in range(half):
        att_o[:, c * LANES : (c + 1) * LANES] = sums[c * seg_dev : (c + 1) * seg_dev, :]
    curv_o[0] = jnp.sum(sums[seg_dev * half : seg_dev * half + 1, :])


def per_device(n_sky, n_tm, tiles, tile_seg, tile_count, src_index, src_coef, obs_weight, att_dir, src_dir):
    td, rows, cols = tiles.shape
    params, src_dev = src_dir.shape
    seg_dev = att_dir.shape[0]
    groups = n_tm // GROUP
    msg = pltpu.VMEM((n_tm * ROWS_MSG, LANES), F32)
    pitch = seg_dev * (cols // LANES) + 8
    vmem, smem, hbm = (
        pl.BlockSpec(memory_space=s) for s in (pltpu.VMEM, pltpu.SMEM, pl.ANY)
    )
    projected, sums, src_normal = pl.pallas_call(
        functools.partial(kernel, n_sky, n_tm),
        out_shape=(
            jax.ShapeDtypeStruct((td, rows), F32),
            jax.ShapeDtypeStruct((pitch, LANES), F32),
            jax.ShapeDtypeStruct((params, src_dev), F32),
        ),
        in_specs=[hbm, hbm, hbm, hbm, hbm, hbm, hbm, hbm],
        out_specs=(vmem, vmem, vmem),
        scratch_shapes=[
            pltpu.SMEM((td,), I32),
            pltpu.SMEM((td,), I32),
            pltpu.VMEM((td, rows, cols), F32),
            pltpu.VMEM((td, rows), I32),
            pltpu.VMEM((params, td, rows), F32),
            pltpu.VMEM((td, rows), F32),
            pltpu.VMEM((seg_dev, cols), F32),
            pltpu.VMEM((params, src_dev), F32),
            pltpu.VMEM((td * rows, cols), BF16),
            pltpu.VMEM((td * rows, cols), BF16),
            pltpu.VMEM((cols, td * rows), BF16),
            pltpu.VMEM((cols, td * rows), BF16),
            pltpu.VMEM((SLOT_T * n_tm, td * rows), BF16),
            pltpu.VMEM((LANES, n_tm * LANES), BF16),
            pltpu.VMEM((td, cols), F32),
            pltpu.VMEM((td, rows), I32),
            pltpu.VMEM((2 * n_tm, LANES), I32),
            msg, msg, msg, msg, msg, msg,
            pltpu.VMEM((pitch, LANES), F32),
            pltpu.VMEM((n_sky * pitch, LANES), F32),
            pltpu.SemaphoreType.DMA((8,)),
            pltpu.SemaphoreType.DMA((4,)),
            pltpu.SemaphoreType.DMA((4, groups)),
            pltpu.SemaphoreType.DMA((1,)),
            pltpu.SemaphoreType.DMA((1,)),
        ],
        compiler_params=pltpu.CompilerParams(
            collective_id=0, has_side_effects=True, vmem_limit_bytes=SCOPED
        ),
    )(
        *[
            pltpu.with_memory_space_constraint(x, pltpu.HBM)
            for x in (
                tile_seg, tile_count, tiles, src_index, src_coef, obs_weight, att_dir, src_dir,
            )
        ]
    )
    projected, att_normal, src_normal, curvature = pl.pallas_call(
        hand_over,
        out_shape=(
            jax.ShapeDtypeStruct((td, rows), F32),
            jax.ShapeDtypeStruct((seg_dev, cols), F32),
            jax.ShapeDtypeStruct((params, src_dev), F32),
            jax.ShapeDtypeStruct((1,), F32),
        ),
        in_specs=[vmem, vmem, vmem],
        out_specs=(vmem, vmem, vmem, smem),
        compiler_params=pltpu.CompilerParams(vmem_limit_bytes=SCOPED),
    )(projected, sums, src_normal)
    return projected, att_normal, src_normal, curvature.reshape(())


def solution(mesh):
    placed = (
        P(("sky", "tm"), None, None),
        P(("sky", "tm")),
        P(("sky", "tm")),
        P(("sky", "tm"), None),
        P(None, ("sky", "tm"), None),
        P(("sky", "tm"), None),
        P("tm", None),
        P(None, ("sky", "tm")),
    )
    return jax.shard_map(
        functools.partial(per_device, mesh.shape["sky"], mesh.shape["tm"]),
        mesh=mesh,
        in_specs=placed,
        out_specs=(P(("sky", "tm"), None), P("tm", None), P(None, ("sky", "tm")), P()),
        check_vma=False,
    )
```

```python
import functools

import jax
import jax.numpy as jnp
from jax import lax
from jax.experimental import pallas as pl
from jax.experimental.pallas import tpu as pltpu
from jax.sharding import PartitionSpec as P

LANES = 128
ROWS_MSG = 8
GROUP = 8
PACKED = 16
SCOPED = 44 << 20
SLOT_T = 2
F32, BF16, I32 = jnp.float32, jnp.bfloat16, jnp.int32
NT = (((1,), (1,)), ((), ()))


def halves(x):
    hi = x.astype(BF16)
    return hi, (x - hi.astype(F32)).astype(BF16)


def iota(shape, dim):
    return lax.broadcasted_iota(I32, shape, dim)


def lanes_of(row, index):
    return jnp.take_along_axis(jnp.broadcast_to(row, index.shape), index, axis=1)


def hops(step, extents):
    total = 0
    for n in reversed(extents):
        part = step % n
        step //= n
        total += min(part, n - part)
    return total


def kernel(
    n_sky, n_tm,
    seg_hbm, cnt_hbm, tiles_hbm, idx_hbm, coef_hbm, wgt_hbm, att_hbm, src_hbm,
    proj_o, sums_o, src_o,
    seg_ref, cnt_ref, tiles_v, idx_v, coef_v, wgt_v, att_v, src_v, thi, tlo, thi_t, tlo_t, slot_v, low_v, dir_v, rank_v, inv_v,
    s1, r1, s2, r2, s3, r3, sz, rz,
    in_sem, send_sem, recv_sem, zsend_sem, zrecv_sem,
):
    params, td, _ = coef_v.shape
    seg_dev, cols = att_v.shape
    src_dev = src_v.shape[1]
    nb = n_tm
    groups = n_tm // GROUP
    chunks = src_dev // LANES
    half = cols // LANES
    me, z = lax.axis_index("tm"), lax.axis_index("sky")
    my_group = me // GROUP
    across = sorted(range(groups), key=lambda k: -min(k, groups - k))
    within = sorted(range(GROUP), key=lambda k: -hops(k, (4, 2)))

    barrier = pltpu.get_barrier_semaphore()

    around = sorted(range(1, n_sky), key=lambda i: -min(i, n_sky - i))
    for i in around:
        pl.semaphore_signal(barrier, 1, device_id=(lax.rem(z + i, n_sky), me))
    for k in across:
        for j in within:
            if k or j:
                q = jnp.bitwise_xor(me, k * GROUP + j)
                pl.semaphore_signal(barrier, 1, device_id=(z, q))

    loads = [
        pltpu.make_async_copy(a, b, in_sem.at[i])
        for i, (a, b) in enumerate(
            ((idx_hbm, idx_v), (coef_hbm, coef_v), (src_hbm, src_v), (att_hbm, att_v),
             (wgt_hbm, wgt_v), (tiles_hbm, tiles_v), (seg_hbm, seg_ref), (cnt_hbm, cnt_ref))
        )
    ]
    for i in (7, 0, 6, 1, 2, 3, 4, 5):
        loads[i].start()

    def strided(ref, row):
        return ref[pl.ds(row, nb, stride=ROWS_MSG), :]

    def put(ref, row, value):
        ref[pl.ds(row, nb, stride=ROWS_MSG), :] = value

    def group_start(k):
        return pl.multiple_of(jnp.bitwise_xor(my_group, k) * (GROUP * ROWS_MSG), GROUP * ROWS_MSG)

    def strided_group(ref, row, k):
        return ref[pl.ds(group_start(k) + row, GROUP, stride=ROWS_MSG), :]

    def put_group(ref, row, k, value):
        ref[pl.ds(group_start(k) + row, GROUP, stride=ROWS_MSG), :] = value

    def block(q, first, rows):
        return pl.ds(pl.multiple_of(q * ROWS_MSG, ROWS_MSG) + first, rows)

    ring = lambda n, extent: min(n, extent - n)
    others = sorted(
        range(1, n_tm),
        key=lambda i: -(ring(i // GROUP, groups) + ring(i % GROUP // 2, GROUP // 2)),
    )

    def send_all(src, dst, phase, first, rows):
        for step in others:
            q = jnp.bitwise_xor(me, step)
            pltpu.make_async_remote_copy(
                src_ref=src.at[block(q, first, rows)], dst_ref=dst.at[block(me, first, rows)],
                send_sem=send_sem.at[phase], recv_sem=recv_sem.at[phase, step // GROUP],
                device_id=(z, q), device_id_type=pl.DeviceIdType.MESH,
            ).start()

    def keep(src, dst):
        dst[block(me, 0, ROWS_MSG), :] = src[block(me, 0, ROWS_MSG), :]

    def await_bytes(ref, rows, sem):
        view = ref.at[pl.ds(0, rows)]
        pltpu.make_async_copy(view, view, sem).wait()

    def await_group(ref, phase, k, rows):
        await_bytes(ref, (GROUP - (k == 0)) * rows, recv_sem.at[phase, k])

    loads[7].wait()
    obs_t, obs_row = iota((td, LANES), 0), iota((td, LANES), 1)
    count = jnp.zeros((td, LANES), I32)
    for t in range(td):
        count = jnp.where(obs_t == t, cnt_ref[t], count)
    live = obs_row < count
    bins, lane = iota((nb, LANES), 0), iota((nb, LANES), 1)
    loads[0].wait()
    src_shift = src_dev.bit_length() - 1
    idx = idx_v[...]
    owner = jnp.where(live, idx >> src_shift, -1)
    mine = [jnp.broadcast_to(owner[t : t + 1], (nb, LANES)) == bins for t in range(td)]
    ones = [m.astype(F32) for m in mine]
    i0, i1 = iota((LANES, 2 * LANES), 0), iota((LANES, 2 * LANES), 1)
    tri = ((i0 < i1) | (i1 >= LANES)).astype(F32).astype(BF16)
    counts = jnp.dot(
        jnp.concatenate(ones, axis=0).astype(BF16), tri, preferred_element_type=F32
    )
    offset = jnp.zeros((nb, LANES), F32)
    slot_id = iota((LANES, LANES), 0)
    spots, origin = [], []
    lane_f = lane.astype(F32)
    for t in range(td):
        here = counts[t * nb : (t + 1) * nb]
        rank = jnp.sum(jnp.where(mine[t], here[:, :LANES] + offset, 0.0), axis=0, keepdims=True)
        rank = rank.astype(I32)
        offset = offset + here[:, LANES:]
        rank_v[t : t + 1, :] = rank
        spots.append((jnp.broadcast_to(rank, (LANES, LANES)) == slot_id).astype(F32).astype(BF16))
        origin.append(jnp.concatenate([ones[t] * (t + 1.0), ones[t] * lane_f], axis=0).astype(BF16))
    found = lax.dot_general(
        jnp.concatenate(origin, axis=1), jnp.concatenate(spots, axis=1), NT,
        preferred_element_type=F32,
    ).astype(I32)
    inv_v[...] = found

    def to_slots(rows):
        tile, col = inv_v[:nb, :], inv_v[nb:, :]
        out = jnp.zeros((nb, LANES), F32)
        for t in range(td):
            out = jnp.where(tile == t + 1, lanes_of(rows[t : t + 1], col), out)
        return out

    loads[1].wait()
    for k in range(params):
        put(s1, k, to_slots(coef_v[k]))
    put(s1, params, to_slots((idx & (src_dev - 1)).astype(F32)))

    loads[6].wait()
    seg_shift = seg_dev.bit_length() - 1
    owner_t = [seg_ref[t] >> seg_shift for t in range(td)]
    local_t = [seg_ref[t] & (seg_dev - 1) for t in range(td)]
    rank_t = []
    for t in range(td):
        r = jnp.int32(0)
        for before in range(t):
            r = r + (owner_t[before] == owner_t[t]).astype(I32)
        rank_t.append(r)
    wanted = jnp.zeros((nb, LANES), I32)
    for t in range(td):
        hit = (bins == owner_t[t]) & (lane == rank_t[t])
        wanted = jnp.where(hit, local_t[t] + 1, wanted)
    put(s1, params + 1, wanted.astype(F32))

    asked_rows = params + 2
    pl.semaphore_wait(barrier, n_tm + n_sky - 2)
    send_all(s1, r1, 0, 0, asked_rows)
    keep(s1, r1)

    n_slots = SLOT_T * nb
    slots = iota((n_slots, LANES), 0)
    for t in range(td):
        slot_v[:, t * LANES : (t + 1) * LANES] = (
            (slots == rank_t[t] * nb + owner_t[t]).astype(F32).astype(BF16)
        )
    loads[5].wait()

    @pl.loop(0, td)
    def _(t):
        rows = pl.ds(pl.multiple_of(t * LANES, LANES), LANES)
        hi, lo = halves(tiles_v[t])
        thi[rows, :] = hi
        tlo[rows, :] = lo
        hi, lo = halves(tiles_v[t].T)
        thi_t[:, rows] = hi
        tlo_t[:, rows] = lo

    for copy in (loads[2], loads[3], loads[4]):
        copy.wait()

    answer_rows = 1 + SLOT_T * half
    @pl.loop(0, groups)
    def _(i):
        k = jnp.bitwise_xor(i, i >> 1)

        @pl.when(i == 0)
        def _():
            await_group(r1, 0, 0, asked_rows)

        @pl.when(i > 0)
        def _():
            await_bytes(r1, GROUP * asked_rows, recv_sem.at[0, k])

        asked = strided_group(r1, params, k).astype(I32)
        chunk, col = asked >> 7, asked & (LANES - 1)
        picked = [jnp.zeros((GROUP, LANES), F32) for _ in range(params)]
        for h in range(chunks):
            here = chunk == h
            for p in range(params):
                row = src_v[p : p + 1, h * LANES : (h + 1) * LANES]
                picked[p] = jnp.where(here, lanes_of(row, col), picked[p])
        total = jnp.zeros((GROUP, LANES), F32)
        for p in range(params):
            total = total + strided_group(r1, p, k) * picked[p]
        put_group(s2, 0, k, total)
        segs = strided_group(r1, params + 1, k).astype(I32)
        for r in range(SLOT_T):
            seg = jnp.broadcast_to(segs[:, r : r + 1], (GROUP, LANES))
            rows = [jnp.zeros((GROUP, LANES), F32) for _ in range(half)]
            for n in range(seg_dev):
                here = seg == n + 1
                for c in range(half):
                    row = att_v[n : n + 1, c * LANES : (c + 1) * LANES]
                    rows[c] = jnp.where(here, jnp.broadcast_to(row, here.shape), rows[c])
            for c in range(half):
                put_group(s2, 1 + r * half + c, k, rows[c])
        for j in within:

            @pl.when((i > 0) | (j > 0))
            def _(j=j):
                q = jnp.bitwise_xor(me, k * GROUP + j)
                pltpu.make_async_remote_copy(
                    src_ref=s2.at[block(q, 0, answer_rows)],
                    dst_ref=r2.at[block(me, 0, answer_rows)],
                    send_sem=send_sem.at[1], recv_sem=recv_sem.at[1, k],
                    device_id=(z, q), device_id_type=pl.DeviceIdType.MESH,
                ).start()

    keep(s2, r2)

    asked = strided(r1, params).astype(I32)
    chunk, col = asked >> 7, asked & (LANES - 1)
    for p in range(nb):
        low_v[:, p * LANES : (p + 1) * LANES] = (
            jnp.broadcast_to(col[p : p + 1], (LANES, LANES)) == slot_id
        ).astype(F32).astype(BF16)
    segs = strided(r1, params + 1).astype(I32)
    choice = jnp.concatenate(
        [
            jnp.broadcast_to(segs[:, r : r + 1], (nb, LANES)) == iota((nb, LANES), 1) + 1
            for r in range(SLOT_T)
        ],
        axis=0,
    ).astype(F32)
    choice = choice.T[:seg_dev].astype(BF16)

    rank = rank_v[...]
    source = jnp.zeros((td, LANES), F32)
    for k in reversed(across):
        await_group(r2, 1, k, answer_rows)
        answers = strided_group(r2, 0, k)
        first = jnp.bitwise_xor(my_group, k) * GROUP
        for w in range(GROUP):
            source = jnp.where(owner == first + w, lanes_of(answers[w : w + 1], rank), source)
    for t in range(td):
        for c in range(half):
            dir_v[t : t + 1, c * LANES : (c + 1) * LANES] = r2[
                pl.ds(owner_t[t] * ROWS_MSG + 1 + rank_t[t] * half + c, 1), :
            ]
    dir_hi, dir_lo = halves(dir_v[...])
    first = jnp.dot(
        jnp.concatenate([dir_hi, dir_lo], axis=0), thi_t[...], preferred_element_type=F32
    )
    second = jnp.dot(dir_hi, tlo_t[...], preferred_element_type=F32)
    sums = first[:td] + first[td:] + second
    part = jnp.zeros((td, LANES), F32)
    for t in range(td):
        part = jnp.where(obs_t == t, sums[:, t * LANES : (t + 1) * LANES], part)
    projected = jnp.where(live, part + source, 0.0)
    proj_o[...] = projected
    weighted = wgt_v[...] * projected
    curvature = jnp.sum(projected * weighted, axis=0, keepdims=True)

    left = []
    for w in halves(weighted):
        w = w.astype(F32)
        spread = [
            jnp.broadcast_to(w[t : t + 1], (PACKED, LANES)).astype(BF16) for t in range(td)
        ]
        row = jnp.concatenate(spread, axis=1)
        left.append(jnp.concatenate([row] * (n_slots // PACKED), axis=0) * slot_v[...])
    left = jnp.concatenate(left, axis=0)
    grad = jnp.dot(left, thi[...], preferred_element_type=F32)
    grad = (
        grad[:n_slots]
        + grad[n_slots:]
        + jnp.dot(left[:n_slots], tlo[...], preferred_element_type=F32)
    )
    for r in range(SLOT_T):
        for c in range(half):
            put(
                s3, r * half + c,
                grad[r * nb : (r + 1) * nb, c * LANES : (c + 1) * LANES],
            )
    curv_row = SLOT_T * half
    put(s3, curv_row, jnp.broadcast_to(curvature, (nb, LANES)))
    send_all(s3, r3, 2, 0, curv_row + 1)
    weight_row = curv_row + 1
    put(s3, weight_row, to_slots(weighted))
    send_all(s3, r3, 3, weight_row, 1)
    keep(s3, r3)
    for k in across:
        await_group(r3, 2, k, curv_row + 1)

    zrows = seg_dev * half + 1
    pitch = rz.shape[0] // n_sky

    def zblock(q):
        return pl.ds(pl.multiple_of(q * pitch, 8), zrows)

    rows = jnp.concatenate(
        [
            jnp.concatenate([strided(r3, r * half + c) for c in range(half)], axis=1)
            for r in range(SLOT_T)
        ],
        axis=0,
    )
    both = jnp.dot(
        choice, jnp.concatenate(halves(rows), axis=1), preferred_element_type=F32
    )
    owned = both[:, :cols] + both[:, cols:]
    for c in range(half):
        sz[c * seg_dev : (c + 1) * seg_dev, :] = owned[:, c * LANES : (c + 1) * LANES]
    sz[zrows - 1 : zrows, :] = jnp.sum(strided(r3, curv_row), axis=0, keepdims=True)

    for i in around:
        q = lax.rem(z + i, n_sky)
        pltpu.make_async_remote_copy(
            src_ref=sz.at[pl.ds(0, zrows)], dst_ref=rz.at[zblock(z)],
            send_sem=zsend_sem.at[0], recv_sem=zrecv_sem.at[0],
            device_id=(q, me), device_id_type=pl.DeviceIdType.MESH,
        ).start()

    rz[zblock(z), :] = sz[0:zrows, :]

    for k in across:
        await_group(r3, 3, k, 1)
    back = strided(r3, weight_row)
    chunk_id = iota((chunks, LANES), 0)
    terms = []
    for k in range(params):
        hi, lo = halves(strided(r1, k) * back)
        terms.append((hi.astype(F32), lo.astype(F32)))
    grid = []
    for p in range(nb):
        here = jnp.broadcast_to(chunk[p : p + 1], chunk_id.shape) == chunk_id
        grid.append(
            jnp.concatenate(
                [
                    jnp.where(here, jnp.broadcast_to(terms[k][i][p : p + 1], here.shape), 0.0)
                    for i in range(2)
                    for k in range(params)
                ],
                axis=0,
            ).astype(BF16)
        )
    both = lax.dot_general(
        jnp.concatenate(grid, axis=1), low_v[...], NT, preferred_element_type=F32
    )
    rows = params * chunks
    spread = both[:rows] + both[rows:]
    for k in range(params):
        for h in range(chunks):
            src_o[k : k + 1, h * LANES : (h + 1) * LANES] = spread[
                k * chunks + h : k * chunks + h + 1
            ]

    for k, (ref, rows) in enumerate(
        ((s1, asked_rows), (s2, answer_rows), (s3, curv_row + 1), (s3, 1))
    ):
        await_bytes(ref, (n_tm - 1) * rows, send_sem.at[k])
    await_bytes(rz, (n_sky - 1) * zrows, zrecv_sem.at[0])
    summed = rz[0:zrows, :]
    for q in range(1, n_sky):
        summed = summed + rz[q * pitch : q * pitch + zrows, :]
    sums_o[0:zrows, :] = summed
    await_bytes(rz, (n_sky - 1) * zrows, zsend_sem.at[0])


def hand_over(proj, sums, src, proj_o, att_o, src_o, curv_o):
    seg_dev, cols = att_o.shape
    half = cols // LANES
    proj_o[...] = proj[...]
    src_o[...] = src[...]
    for c in range(half):
        att_o[:, c * LANES : (c + 1) * LANES] = sums[c * seg_dev : (c + 1) * seg_dev, :]
    curv_o[0] = jnp.sum(sums[seg_dev * half : seg_dev * half + 1, :])


def per_device(n_sky, n_tm, tiles, tile_seg, tile_count, src_index, src_coef, obs_weight, att_dir, src_dir):
    td, rows, cols = tiles.shape
    params, src_dev = src_dir.shape
    seg_dev = att_dir.shape[0]
    groups = n_tm // GROUP
    msg = pltpu.VMEM((n_tm * ROWS_MSG, LANES), F32)
    pitch = seg_dev * (cols // LANES) + 8
    vmem, smem, hbm = (
        pl.BlockSpec(memory_space=s) for s in (pltpu.VMEM, pltpu.SMEM, pl.ANY)
    )
    projected, sums, src_normal = pl.pallas_call(
        functools.partial(kernel, n_sky, n_tm),
        out_shape=(
            jax.ShapeDtypeStruct((td, rows), F32),
            jax.ShapeDtypeStruct((pitch, LANES), F32),
            jax.ShapeDtypeStruct((params, src_dev), F32),
        ),
        in_specs=[hbm, hbm, hbm, hbm, hbm, hbm, hbm, hbm],
        out_specs=(vmem, vmem, vmem),
        scratch_shapes=[
            pltpu.SMEM((td,), I32),
            pltpu.SMEM((td,), I32),
            pltpu.VMEM((td, rows, cols), F32),
            pltpu.VMEM((td, rows), I32),
            pltpu.VMEM((params, td, rows), F32),
            pltpu.VMEM((td, rows), F32),
            pltpu.VMEM((seg_dev, cols), F32),
            pltpu.VMEM((params, src_dev), F32),
            pltpu.VMEM((td * rows, cols), BF16),
            pltpu.VMEM((td * rows, cols), BF16),
            pltpu.VMEM((cols, td * rows), BF16),
            pltpu.VMEM((cols, td * rows), BF16),
            pltpu.VMEM((SLOT_T * n_tm, td * rows), BF16),
            pltpu.VMEM((LANES, n_tm * LANES), BF16),
            pltpu.VMEM((td, cols), F32),
            pltpu.VMEM((td, rows), I32),
            pltpu.VMEM((2 * n_tm, LANES), I32),
            msg, msg, msg, msg, msg, msg,
            pltpu.VMEM((pitch, LANES), F32),
            pltpu.VMEM((n_sky * pitch, LANES), F32),
            pltpu.SemaphoreType.DMA((8,)),
            pltpu.SemaphoreType.DMA((4,)),
            pltpu.SemaphoreType.DMA((4, groups)),
            pltpu.SemaphoreType.DMA((1,)),
            pltpu.SemaphoreType.DMA((1,)),
        ],
        compiler_params=pltpu.CompilerParams(
            collective_id=0, has_side_effects=True, vmem_limit_bytes=SCOPED
        ),
    )(
        *[
            pltpu.with_memory_space_constraint(x, pltpu.HBM)
            for x in (
                tile_seg, tile_count, tiles, src_index, src_coef, obs_weight, att_dir, src_dir,
            )
        ]
    )
    projected, att_normal, src_normal, curvature = pl.pallas_call(
        hand_over,
        out_shape=(
            jax.ShapeDtypeStruct((td, rows), F32),
            jax.ShapeDtypeStruct((seg_dev, cols), F32),
            jax.ShapeDtypeStruct((params, src_dev), F32),
            jax.ShapeDtypeStruct((1,), F32),
        ),
        in_specs=[vmem, vmem, vmem],
        out_specs=(vmem, vmem, vmem, smem),
        compiler_params=pltpu.CompilerParams(vmem_limit_bytes=SCOPED),
    )(projected, sums, src_normal)
    return projected, att_normal, src_normal, curvature.reshape(())


def solution(mesh):
    placed = (
        P(("sky", "tm"), None, None),
        P(("sky", "tm")),
        P(("sky", "tm")),
        P(("sky", "tm"), None),
        P(None, ("sky", "tm"), None),
        P(("sky", "tm"), None),
        P("tm", None),
        P(None, ("sky", "tm")),
    )
    return jax.shard_map(
        functools.partial(per_device, mesh.shape["sky"], mesh.shape["tm"]),
        mesh=mesh,
        in_specs=placed,
        out_specs=(P(("sky", "tm"), None), P("tm", None), P(None, ("sky", "tm")), P()),
        check_vma=False,
    )
```
